32 devices in a mesh: section: 4 (over y, x), sta: 8 (over z, core).
Axes of the slice: x: 2, y: 2, z: 4, core: 2. Of those that a mesh axis runs over, the one named last changes fastest.
Arguments:
- waveforms: bfloat16 [4, 64, 8, 4096], P('section', 'sta'), may hold values from -6 to 6
- segment_mask: int32 [4, 64, 8], P('section', 'sta'), may hold values 0 or 1
- pair_blocks: int32 [8, 4], P('sta'), may hold values from 0 to 7, as said below
- window_decay: float32 [4], P('section'), may hold values from 0.5 to 1
Outputs:
- stacked: bfloat16 [4, 64, 32, 384], P('section', 'sta')
The draws below stay inside these ranges and needn't reach their ends.
Inputs may be any that keep to these rules, and one draw needn't show every extreme that they name: `pair_blocks`: entry k of row b names a block of 8 stations other than b; entries of a row may repeat.
All inputs are finite; a program needn't handle non-finite values. No bound on the sum of `segment_mask` on one device may be relied on, other than what follows from the above.
Results may differ from the reference program's by a relative error of at most 0.008.
Values may be sent and summed in bfloat16 or wider, within the bound.
A program may use at most 64 MiB of HBM per device.

```python
import math
import jax
import jax.numpy as jnp
from jax import lax

RADIX = 64
NF = 1024
LAGS = 384
SMOOTH_HALF = 32
PB = 4
LS = 8
SEGS = 8
NSAMP = 4096
BLOCKS = 8
STATIONS = 64
PARTNERS = 32
WINDOWS = 4


def draw_pair_blocks(key, part):
    offsets = jax.random.randint(key, (BLOCKS, PB), 1, BLOCKS)
    block_ids = jnp.arange(BLOCKS, dtype=jnp.int32)[:, None]
    return ((block_ids + offsets) % BLOCKS).astype(jnp.int32)


def plant(drawn, rng, low, high):
    spot = [jax.random.randint(jax.random.fold_in(rng, axis), (), 0, length) for axis, length in enumerate(drawn.shape)]
    widest = drawn.shape.index(max(drawn.shape))
    beside = spot[:widest] + [(spot[widest] + 1) % drawn.shape[widest]] + spot[widest + 1:]
    return drawn.at[tuple(spot)].set(low).at[tuple(beside)].set(high)


def block_scale(own_key, shape, shards, least, top_value):
    level = 1.0
    for dim, blocks in shards:
        heights = jax.random.uniform(jax.random.fold_in(jax.random.fold_in(own_key, 6), dim), (blocks,), jnp.float32, least / len(shards), top_value / len(shards))
        level = level * jnp.repeat(jnp.exp(heights), shape[dim] // blocks).reshape((-1,) + (1,) * (len(shape) - 1 - dim))
    return level


def centred(rng, extent, deviation, reach, shards=(), held_as=jnp.bfloat16):
    drawn = deviation * jax.random.normal(rng, extent, jnp.float32)
    if shards:
        drawn = drawn * block_scale(rng, extent, shards, -0.22, 0.18)
    return jnp.clip(drawn, -reach, reach).astype(held_as)


def setup_inputs(seed: int = 0) -> dict:
    streams_of = jax.random.split(jax.random.key(seed), 5)
    return {
        "waveforms": centred(streams_of[0], (WINDOWS, STATIONS, SEGS, NSAMP), 1.0, 6.0, ((0, 4), (1, 8))),
        "segment_mask": plant((jax.random.randint(streams_of[1], (WINDOWS, STATIONS, SEGS), 0, 2) < 1).astype(jnp.int32), jax.random.fold_in(streams_of[1], 1), 0, 1),
        "pair_blocks": draw_pair_blocks(jax.random.fold_in(streams_of[4], 71), 0),
        "window_decay": jnp.clip(0.5 + 0.5 * jax.random.uniform(streams_of[3], (WINDOWS,), jnp.float32) ** block_scale(streams_of[3], (WINDOWS,), ((0, 4),), -0.2, 0.2), 0.5, 1.0),
    }


epsilon = 1e-05

def band_spectrum(waves):
    spectrum = jnp.fft.rfft(waves.astype(jnp.float32), axis=-1)
    lowest = 2 * RADIX
    spectrum = spectrum[..., lowest:lowest + NF] / RADIX
    return (jnp.real(spectrum), jnp.imag(spectrum))

def whiten(spec_real, spec_imag):
    amplitude = jnp.sqrt(spec_real * spec_real + spec_imag * spec_imag)
    widths = [(0, 0)] * (amplitude.ndim - 1) + [(SMOOTH_HALF, SMOOTH_HALF)]
    padded = jnp.pad(amplitude, widths)
    smooth = jnp.zeros_like(amplitude)
    for offset in range(2 * SMOOTH_HALF + 1):
        smooth = smooth + padded[..., offset:offset + NF]
    smooth = smooth / (2 * SMOOTH_HALF + 1)
    white_real = (spec_real / (smooth + epsilon)).astype(jnp.bfloat16)
    white_imag = (spec_imag / (smooth + epsilon)).astype(jnp.bfloat16)
    return (white_real, white_imag)

def lag_table():
    freq_bins = 2 * RADIX + jnp.arange(NF, dtype=jnp.int32)
    lag_shift = jnp.arange(LAGS, dtype=jnp.int32) + RADIX * RADIX - LAGS // 2
    phase = (freq_bins[:, None] * lag_shift[None, :] % (RADIX * RADIX)).astype(jnp.float32) * (2.0 * jnp.pi / (RADIX * RADIX))
    table = jnp.concatenate([jnp.cos(phase), -jnp.sin(phase)], axis=0) / math.sqrt(NF)
    return table.astype(jnp.bfloat16)

def correlate(local_real, local_imag, local_marks, part_real, part_imag, part_marks, table):
    mine_real = local_real.astype(jnp.float32) * local_marks[:, :, None]
    mine_imag = local_imag.astype(jnp.float32) * local_marks[:, :, None]
    other_real = part_real.astype(jnp.float32) * part_marks[:, :, None]
    other_imag = part_imag.astype(jnp.float32) * part_marks[:, :, None]
    cross_real = jnp.einsum('isf,jsf->ijf', mine_real, other_real) + jnp.einsum('isf,jsf->ijf', mine_imag, other_imag)
    cross_imag = jnp.einsum('isf,jsf->ijf', mine_real, other_imag) - jnp.einsum('isf,jsf->ijf', mine_imag, other_real)
    count = jnp.einsum('is,js->ij', local_marks, part_marks)
    divisor = jnp.maximum(count, 1.0)[:, :, None]
    cross = (jnp.concatenate([cross_real, cross_imag], axis=-1) / divisor).astype(jnp.bfloat16)
    lagged = jnp.dot(cross.reshape(-1, 2 * NF), table, preferred_element_type=jnp.float32)
    return lagged.reshape(local_real.shape[0], part_real.shape[0], LAGS)

def reference(waveforms, segment_mask, pair_blocks, window_decay):
    table = lag_table()

    def one_window(state, inputs):
        waves, marks, decay = inputs
        spec_real, spec_imag = band_spectrum(waves)
        white_real, white_imag = whiten(spec_real, spec_imag)
        marks = marks.astype(jnp.float32)
        blocks_real = white_real.reshape(BLOCKS, LS, SEGS, NF)
        blocks_imag = white_imag.reshape(BLOCKS, LS, SEGS, NF)
        blocks_marks = marks.reshape(BLOCKS, LS, SEGS)

        def per_block(items):
            local_real, local_imag, local_marks, chosen = items
            part_real = jnp.take(blocks_real, chosen, axis=0).reshape(PB * LS, SEGS, NF)
            part_imag = jnp.take(blocks_imag, chosen, axis=0).reshape(PB * LS, SEGS, NF)
            part_marks = jnp.take(blocks_marks, chosen, axis=0).reshape(PB * LS, SEGS)
            return correlate(local_real, local_imag, local_marks, part_real, part_imag, part_marks, table)
        lagged = lax.map(per_block, (blocks_real, blocks_imag, blocks_marks, pair_blocks))
        lagged = lagged.reshape(STATIONS, PARTNERS, LAGS)
        state = decay * state + lagged
        return (state, state.astype(jnp.bfloat16))
    initial = jnp.zeros((STATIONS, PARTNERS, LAGS), jnp.float32)
    final_state, stacked = lax.scan(one_window, initial, (waveforms, segment_mask, window_decay))
    return stacked
```

```python
import functools
import math

import jax
import jax.numpy as jnp
import numpy as np
from jax import lax
from jax.experimental import pallas as pl
from jax.experimental.pallas import tpu as pltpu
from jax.sharding import PartitionSpec as P

MESH = pl.DeviceIdType.MESH
RADIX = 64
NF = 1024
LAGS = 384
SMOOTH_HALF = 32
LANES = 128
SUB = 8
EPSILON = 1e-05
NSAMP = RADIX * RADIX
FIRST = NSAMP // LANES
SLICES = FIRST // SUB
BINS = NF // FIRST


def dft_tables():
    b = np.arange(LANES)
    m = np.arange(BINS)
    phi = 2.0 * np.pi * ((b[:, None] * (m[None, :] + 2 * RADIX // FIRST)) % LANES) / LANES
    table = np.zeros((SLICES, 2, LANES, 2, BINS, SLICES))
    for q in range(SLICES):
        table[q, 0, :, 0, :, q] = np.cos(phi)
        table[q, 1, :, 0, :, q] = np.sin(phi)
        table[q, 0, :, 1, :, q] = -np.sin(phi)
        table[q, 1, :, 1, :, q] = np.cos(phi)
    table = (table / RADIX).reshape(SLICES * 2 * LANES, 2 * BINS * SLICES).astype(np.float32)
    high = table.astype(jnp.bfloat16)
    low = (table - high.astype(np.float32)).astype(jnp.bfloat16)
    turn = 2.0 * np.pi * np.arange(FIRST)[:, None] * b[None, :] / NSAMP
    twist = np.stack([np.cos(turn), np.sin(turn)], axis=1).astype(np.float32)
    return high, low, twist


def lag_table():
    f = SUB * np.arange(NF // SUB)[None, :] + np.arange(SUB)[:, None]
    shift = np.arange(LAGS) + NSAMP - LAGS // 2
    theta = 2.0 * np.pi * (((2 * RADIX + f)[:, :, None] * shift) % NSAMP) / NSAMP
    table = np.concatenate([np.cos(theta), -np.sin(theta)], axis=1) / math.sqrt(NF)
    return table.astype(np.float32).astype(jnp.bfloat16)


def real_dft(values):
    size = len(values)
    if size == 1:
        return [(values[0], None)]
    if size == 2:
        return [(values[0] + values[1], None), (values[0] - values[1], None)]
    even, odd = real_dft(values[0::2]), real_dft(values[1::2])
    half = size // 2
    out = [None] * (half + 1)
    for k in range(half // 2 + 1):
        er, ei = even[k]
        pr, pi = odd[k]
        if k == 0:
            out[0] = (er + pr, None)
            out[half] = (er - pr, None)
            continue
        if k * 4 == size:
            out[k] = (er, -pr)
            continue
        c, s = math.cos(2 * math.pi * k / size), math.sin(2 * math.pi * k / size)
        tr, ti = pr * c + pi * s, pi * c - pr * s
        out[k] = (er + tr, ei + ti)
        out[half - k] = (er - tr, ti - ei)
    return out


def spectrum_kernel(stations, x_ref, mask_ref, row_ref, high_ref, low_ref, twist_ref, out_ref, y_ref, z_ref, w_ref):
    rows = stations * SUB

    def first(st, _):
        pieces = [x_ref[0, st, :, a * LANES:(a + 1) * LANES].astype(jnp.float32) for a in range(FIRST)]
        spread = real_dft(pieces)
        base = pl.multiple_of(st * SUB, SUB)
        for k1 in range(FIRST):
            re, im = spread[k1] if 2 * k1 <= FIRST else spread[FIRST - k1]
            c, s = twist_ref[k1, 0:1, :], twist_ref[k1, 1:2, :]
            if im is None:
                yr, yi = re * c, -(re * s)
            elif 2 * k1 <= FIRST:
                yr, yi = re * c + im * s, im * c - re * s
            else:
                yr, yi = re * c - im * s, -(im * c) - re * s
            q, p = k1 // SUB, k1 % SUB
            y_ref[pl.ds(p * rows + base, SUB), 2 * q * LANES:(2 * q + 1) * LANES] = yr
            y_ref[pl.ds(p * rows + base, SUB), (2 * q + 1) * LANES:(2 * q + 2) * LANES] = yi
        return 0

    lax.fori_loop(0, stations, first, 0)
    y = y_ref[...]
    yh = y.astype(jnp.bfloat16)
    yl = (y - yh.astype(jnp.float32)).astype(jnp.bfloat16)
    dot = functools.partial(jnp.dot, preferred_element_type=jnp.float32)
    z_ref[...] = dot(yh, high_ref[...]) + dot(yl, high_ref[...]) + dot(yh, low_ref[...])
    reach = SMOOTH_HALF // SUB

    def second(st, _):
        base = pl.multiple_of(st * SUB, SUB)
        lane = lax.broadcasted_iota(jnp.int32, (SUB, LANES), 1)

        def moved(v, d):
            inside = (lane + d >= 0) & (lane + d < LANES)
            return jnp.where(inside, pltpu.roll(v, (-d) % LANES, 1), 0.0)

        re = [z_ref[pl.ds(p * rows + base, SUB), 0:LANES] for p in range(SUB)]
        im = [z_ref[pl.ds(p * rows + base, SUB), LANES:2 * LANES] for p in range(SUB)]
        amp = [jnp.sqrt(re[p] * re[p] + im[p] * im[p]) for p in range(SUB)]
        pre = [amp[0]]
        for p in range(1, SUB):
            pre.append(pre[-1] + amp[p])
        suf = [amp[SUB - 1]]
        for p in range(SUB - 2, -1, -1):
            suf.insert(0, suf[0] + amp[p])
        middle = pre[-1]
        for d in range(1, reach):
            middle = middle + moved(pre[-1], d) + moved(pre[-1], -d)
        marks = mask_ref[st]
        for p in range(SUB):
            smooth = (middle + moved(suf[p], -reach) + moved(pre[p], reach)) / (2 * SMOOTH_HALF + 1)
            scale = marks / (smooth + EPSILON)
            w_ref[pl.ds(p, SUB, stride=2 * SUB), :] = re[p] * scale
            w_ref[pl.ds(SUB + p, SUB, stride=2 * SUB), :] = im[p] * scale
        out_ref[pl.ds(base, SUB)] = w_ref[...].reshape(SUB, 2 * SUB, LANES).astype(jnp.bfloat16)
        return 0

    lax.fori_loop(0, stations, second, 0)
    out_ref[rows] = row_ref[...]


def gather_kernel(n, own_ref, all_ref, send_sem, recv_sem, cross_send, cross_recv):
    me = lax.axis_index("sta")
    ring = n // 2
    core, place = lax.rem(me, 2), me // 2
    right = lax.rem(place + 1, ring) * 2 + core
    left = lax.rem(place + ring - 1, ring) * 2 + core
    mate = place * 2 + 1 - core
    barrier = pltpu.get_barrier_semaphore()
    peers = [mate, right, left]
    for peer in peers:
        pl.semaphore_signal(barrier, inc=1, device_id={"sta": peer}, device_id_type=MESH)
    pl.semaphore_wait(barrier, len(peers))
    count = own_ref.shape[0]
    cut = count // 2

    def block(step):
        return lax.rem(place + step + 2 * ring, ring) * 2 + core

    def remote(src, dst, i, sems, peer):
        return pltpu.make_async_remote_copy(
            src_ref=src, dst_ref=dst, send_sem=sems[0].at[i], recv_sem=sems[1].at[i],
            device_id={"sta": peer}, device_id_type=MESH,
        )

    rail, inner = (send_sem, recv_sem), (cross_send, cross_recv)
    started = []

    def go(src, dst, i, sems, peer):
        copy = remote(src, dst, i, sems, peer)
        copy.start()
        started.append(copy)
        return copy

    to_right = go(own_ref, all_ref.at[me], 0, rail, right)
    to_left = go(own_ref, all_ref.at[me], 1, rail, left)
    inward = [go(own_ref, all_ref.at[me], 0, inner, mate)]
    slot = 1
    half = ring // 2
    for distance in range(1, half + 1):
        from_left, from_right = block(-distance), block(distance)
        to_right.wait_recv()
        if distance < half:
            to_left.wait_recv()
            if distance + 1 < half:
                to_right = go(all_ref.at[from_left], all_ref.at[from_left], 2 * distance, rail, right)
                to_left = go(all_ref.at[from_right], all_ref.at[from_right], 2 * distance + 1, rail, left)
            else:
                first = pl.ds(0, cut)
                rest = pl.ds(cut, count - cut)
                to_right = go(all_ref.at[from_left, first], all_ref.at[from_left, first], 2 * distance, rail, right)
                to_left = go(all_ref.at[from_right, rest], all_ref.at[from_right, rest], 2 * distance + 1, rail, left)
            inward.append(go(all_ref.at[from_left], all_ref.at[from_left], slot, inner, mate))
            inward.append(go(all_ref.at[from_right], all_ref.at[from_right], slot + 1, inner, mate))
            slot += 2
        else:
            if half > 1:
                to_left.wait_recv()
            else:
                to_left.wait_recv()
            inward.append(go(all_ref.at[from_left], all_ref.at[from_left], slot, inner, mate))
    for copy in inward:
        copy.wait_recv()
    for copy in started:
        copy.wait_send()


def cross_kernel(stations, slots, pair_ref, own_ref, all_ref, table_ref, lag_ref, send_ref, loc_ref, cr_ref, ci_ref):
    segments = SUB
    total = stations * slots * stations
    loc_ref[...] = own_ref[0:stations * segments].astype(jnp.float32)

    def pair(kj, _):
        k, j = kj // stations, lax.rem(kj, stations)
        block = pair_ref[0, k]
        other = [all_ref[block, j * segments + s].astype(jnp.float32) for s in range(segments)]
        for i in range(stations):
            re = im = None
            for s in range(segments):
                ar, ai = loc_ref[i * segments + s, 0:SUB, :], loc_ref[i * segments + s, SUB:2 * SUB, :]
                br, bi = other[s][0:SUB], other[s][SUB:2 * SUB]
                tr, ti = ar * br + ai * bi, ar * bi - ai * br
                re, im = (tr, ti) if re is None else (re + tr, im + ti)
            at = pl.ds(pl.multiple_of((i * slots * stations + kj) * SUB, SUB), SUB)
            cr_ref[at, :] = re
            ci_ref[at, :] = im
        return 0

    lax.fori_loop(0, slots * stations, pair, 0)
    acc = None
    for p in range(SUB):
        at = pl.ds(p, total, stride=SUB)
        lhs = jnp.concatenate([cr_ref[at, :], ci_ref[at, :]], axis=1).astype(jnp.bfloat16)
        term = jnp.dot(lhs, table_ref[p], preferred_element_type=jnp.float32)
        acc = term if acc is None else acc + term
    mine = own_ref[stations * segments].astype(jnp.float32)
    for k in range(slots):
        theirs = all_ref[pair_ref[0, k], stations * segments].astype(jnp.float32)[0:stations]
        for i in range(stations):
            count = jnp.sum(mine[i:i + 1] * theirs, axis=1, keepdims=True)
            at = (i * slots + k) * stations
            value = acc[at:at + stations] / jnp.maximum(count, 1.0)
            lag_ref[at:at + stations, :] = value
    send_ref[...] = lag_ref[...].astype(jnp.bfloat16)


def stack_kernel(windows, lag_ref, send_ref, decay_ref, out_ref, got_ref, rate_ref, acc_ref, send_sem, recv_sem, rate_send, rate_recv):
    me = lax.axis_index("section")
    barrier = pltpu.get_barrier_semaphore()
    for d in range(1, windows):
        pl.semaphore_signal(barrier, inc=1, device_id={"section": lax.rem(me + d, windows)}, device_id_type=MESH)
    pl.semaphore_wait(barrier, windows - 1)

    def copies(source, target):
        peer = {"section": target}
        return (
            pltpu.make_async_remote_copy(
                src_ref=send_ref, dst_ref=got_ref.at[source], send_sem=send_sem.at[target],
                recv_sem=recv_sem.at[source], device_id=peer, device_id_type=MESH),
            pltpu.make_async_remote_copy(
                src_ref=decay_ref, dst_ref=rate_ref.at[source], send_sem=rate_send.at[target],
                recv_sem=rate_recv.at[source], device_id=peer, device_id_type=MESH),
        )

    for d in range(1, windows):
        @pl.when(me + d < windows)
        def _():
            for copy in copies(me, me + d):
                copy.start()
    acc_ref[...] = jnp.zeros_like(acc_ref)
    for v in range(windows - 1):
        @pl.when(v < me)
        def _():
            for copy in copies(v, me):
                copy.wait_recv()
            acc_ref[...] = acc_ref[...] * rate_ref[v, 0:1, 0:1] + got_ref[v].astype(jnp.float32)
    out_ref[...] = (acc_ref[...] * decay_ref[0:1, 0:1] + lag_ref[...]).astype(jnp.bfloat16)
    for d in range(1, windows):
        @pl.when(me + d < windows)
        def _():
            for copy in copies(me, me + d):
                copy.wait_send()


def body(sizes, waveforms, segment_mask, pair_blocks, window_decay):
    n, windows = sizes
    stations, segments = waveforms.shape[1], waveforms.shape[2]
    slots = pair_blocks.shape[1]
    rows = stations * segments
    marks = segment_mask[0].astype(jnp.float32)
    marks_wide = jnp.broadcast_to(marks[:, :, None], (stations, segments, LANES))
    marks_row = jnp.pad(marks, ((0, 2 * SUB - stations), (0, LANES - segments))).astype(jnp.bfloat16)
    high, low, twist = dft_tables()
    vmem = pl.BlockSpec(memory_space=pltpu.VMEM)
    smem = pl.BlockSpec(memory_space=pltpu.SMEM)
    tile = (rows + 1, 2 * SUB, LANES)
    own = pl.pallas_call(
        functools.partial(spectrum_kernel, stations),
        name="spectrum",
        out_shape=jax.ShapeDtypeStruct(tile, jnp.bfloat16),
        in_specs=[vmem] * 6,
        out_specs=vmem,
        scratch_shapes=[
            pltpu.VMEM((SUB * rows, SLICES * 2 * LANES), jnp.float32),
            pltpu.VMEM((SUB * rows, 2 * LANES), jnp.float32),
            pltpu.VMEM((SUB * 2 * SUB, LANES), jnp.float32),
        ],
    )(waveforms, marks_wide, marks_row, jnp.asarray(high), jnp.asarray(low), jnp.asarray(twist))
    dma = pltpu.SemaphoreType.DMA
    gathered = pl.pallas_call(
        functools.partial(gather_kernel, n),
        name="gather",
        out_shape=jax.ShapeDtypeStruct((n,) + tile, jnp.bfloat16),
        in_specs=[vmem],
        out_specs=vmem,
        scratch_shapes=[dma((n,)), dma((n,)), dma((n,)), dma((n,))],
        compiler_params=pltpu.CompilerParams(collective_id=0, has_side_effects=True),
    )(own)
    total = stations * slots * stations
    lagged, sent = pl.pallas_call(
        functools.partial(cross_kernel, stations, slots),
        name="cross",
        out_shape=(
            jax.ShapeDtypeStruct((total, LAGS), jnp.float32),
            jax.ShapeDtypeStruct((total, LAGS), jnp.bfloat16),
        ),
        in_specs=[smem, vmem, vmem, vmem],
        out_specs=(vmem, vmem),
        scratch_shapes=[
            pltpu.VMEM((rows, 2 * SUB, LANES), jnp.float32),
            pltpu.VMEM((total * SUB, LANES), jnp.float32),
            pltpu.VMEM((total * SUB, LANES), jnp.float32),
        ],
    )(pair_blocks, own, gathered, jnp.asarray(lag_table()))
    decay = jnp.broadcast_to(window_decay[:, None], (SUB, LANES))
    stacked = pl.pallas_call(
        functools.partial(stack_kernel, windows),
        name="stack",
        out_shape=jax.ShapeDtypeStruct((total, LAGS), jnp.bfloat16),
        in_specs=[vmem] * 3,
        out_specs=vmem,
        scratch_shapes=[
            pltpu.VMEM((windows, total, LAGS), jnp.bfloat16),
            pltpu.VMEM((windows, SUB, LANES), jnp.float32),
            pltpu.VMEM((total, LAGS), jnp.float32),
            dma((windows,)), dma((windows,)), dma((windows,)), dma((windows,)),
        ],
        compiler_params=pltpu.CompilerParams(collective_id=1, has_side_effects=True),
    )(lagged, sent, decay)
    return stacked.reshape(1, stations, slots * stations, LAGS)


def solution(mesh):
    in_specs = (
        P("section", "sta", None, None),
        P("section", "sta", None),
        P("sta", None),
        P("section"),
    )
    out_specs = P("section", "sta", None, None)
    sizes = (mesh.shape["sta"], mesh.shape["section"])
    return jax.shard_map(
        functools.partial(body, sizes), mesh=mesh, in_specs=in_specs, out_specs=out_specs, check_vma=False
    )
```

```python
import functools
import math

import jax
import jax.numpy as jnp
import numpy as np
from jax import lax
from jax.experimental import pallas as pl
from jax.experimental.pallas import tpu as pltpu
from jax.sharding import PartitionSpec as P

MESH = pl.DeviceIdType.MESH
RADIX = 64
NF = 1024
LAGS = 384
SMOOTH_HALF = 32
LANES = 128
SUB = 8
EPSILON = 1e-05
NSAMP = RADIX * RADIX
FIRST = NSAMP // LANES
SLICES = FIRST // SUB
BINS = NF // FIRST


def dft_tables():
    b = np.arange(LANES)
    m = np.arange(BINS)
    phi = 2.0 * np.pi * ((b[:, None] * (m[None, :] + 2 * RADIX // FIRST)) % LANES) / LANES
    table = np.zeros((SLICES, 2, LANES, 2, BINS, SLICES))
    for q in range(SLICES):
        table[q, 0, :, 0, :, q] = np.cos(phi)
        table[q, 1, :, 0, :, q] = np.sin(phi)
        table[q, 0, :, 1, :, q] = -np.sin(phi)
        table[q, 1, :, 1, :, q] = np.cos(phi)
    table = (table / RADIX).reshape(SLICES * 2 * LANES, 2 * BINS * SLICES).astype(np.float32)
    high = table.astype(jnp.bfloat16)
    low = (table - high.astype(np.float32)).astype(jnp.bfloat16)
    turn = 2.0 * np.pi * np.arange(FIRST)[:, None] * b[None, :] / NSAMP
    twist = np.stack([np.cos(turn), np.sin(turn)], axis=1).astype(np.float32)
    return high, low, twist


def lag_table():
    f = SUB * np.arange(NF // SUB)[None, :] + np.arange(SUB)[:, None]
    shift = np.arange(LAGS) + NSAMP - LAGS // 2
    theta = 2.0 * np.pi * (((2 * RADIX + f)[:, :, None] * shift) % NSAMP) / NSAMP
    table = np.concatenate([np.cos(theta), -np.sin(theta)], axis=1) / math.sqrt(NF)
    return table.astype(np.float32).astype(jnp.bfloat16)


def real_dft(values):
    size = len(values)
    if size == 1:
        return [(values[0], None)]
    if size == 2:
        return [(values[0] + values[1], None), (values[0] - values[1], None)]
    even, odd = real_dft(values[0::2]), real_dft(values[1::2])
    half = size // 2
    out = [None] * (half + 1)
    for k in range(half // 2 + 1):
        er, ei = even[k]
        pr, pi = odd[k]
        if k == 0:
            out[0] = (er + pr, None)
            out[half] = (er - pr, None)
            continue
        if k * 4 == size:
            out[k] = (er, -pr)
            continue
        c, s = math.cos(2 * math.pi * k / size), math.sin(2 * math.pi * k / size)
        tr, ti = pr * c + pi * s, pi * c - pr * s
        out[k] = (er + tr, ei + ti)
        out[half - k] = (er - tr, ti - ei)
    return out


def spectrum_kernel(stations, x_ref, mask_ref, high_ref, low_ref, twist_ref, out_ref, y_ref, z_ref, w_ref, row_ref):
    rows = stations * SUB

    def first(st, _):
        pieces = [x_ref[0, st, :, a * LANES:(a + 1) * LANES].astype(jnp.float32) for a in range(FIRST)]
        spread = real_dft(pieces)
        base = pl.multiple_of(st * SUB, SUB)
        for k1 in range(FIRST):
            re, im = spread[k1] if 2 * k1 <= FIRST else spread[FIRST - k1]
            c, s = twist_ref[k1, 0:1, :], twist_ref[k1, 1:2, :]
            if im is None:
                yr, yi = re * c, -(re * s)
            elif 2 * k1 <= FIRST:
                yr, yi = re * c + im * s, im * c - re * s
            else:
                yr, yi = re * c - im * s, -(im * c) - re * s
            q, p = k1 // SUB, k1 % SUB
            y_ref[pl.ds(p * rows + base, SUB), 2 * q * LANES:(2 * q + 1) * LANES] = yr
            y_ref[pl.ds(p * rows + base, SUB), (2 * q + 1) * LANES:(2 * q + 2) * LANES] = yi
        return 0

    lax.fori_loop(0, stations, first, 0)
    y = y_ref[...]
    yh = y.astype(jnp.bfloat16)
    yl = (y - yh.astype(jnp.float32)).astype(jnp.bfloat16)
    dot = functools.partial(jnp.dot, preferred_element_type=jnp.float32)
    z_ref[...] = dot(yh, high_ref[...]) + dot(yl, high_ref[...]) + dot(yh, low_ref[...])
    reach = SMOOTH_HALF // SUB
    square = lax.broadcasted_iota(jnp.int32, (SUB, SUB), 0) == lax.broadcasted_iota(jnp.int32, (SUB, SUB), 1)

    def second(st, _):
        base = pl.multiple_of(st * SUB, SUB)
        lane = lax.broadcasted_iota(jnp.int32, (SUB, LANES), 1)

        def moved(v, d):
            inside = (lane + d >= 0) & (lane + d < LANES)
            return jnp.where(inside, pltpu.roll(v, (-d) % LANES, 1), 0.0)

        re = [z_ref[pl.ds(p * rows + base, SUB), 0:LANES] for p in range(SUB)]
        im = [z_ref[pl.ds(p * rows + base, SUB), LANES:2 * LANES] for p in range(SUB)]
        amp = [jnp.sqrt(re[p] * re[p] + im[p] * im[p]) for p in range(SUB)]
        pre = [amp[0]]
        for p in range(1, SUB):
            pre.append(pre[-1] + amp[p])
        suf = [amp[SUB - 1]]
        for p in range(SUB - 2, -1, -1):
            suf.insert(0, suf[0] + amp[p])
        middle = pre[-1]
        for d in range(1, reach):
            middle = middle + moved(pre[-1], d) + moved(pre[-1], -d)
        row = jnp.broadcast_to(mask_ref[0, pl.ds(st, 1), :].astype(jnp.float32), (SUB, SUB))
        marks = jnp.sum(jnp.where(square, row, 0.0), axis=1, keepdims=True)
        for p in range(SUB):
            smooth = (middle + moved(suf[p], -reach) + moved(pre[p], reach)) / (2 * SMOOTH_HALF + 1)
            scale = marks / (smooth + EPSILON)
            w_ref[pl.ds(p, SUB, stride=2 * SUB), :] = re[p] * scale
            w_ref[pl.ds(SUB + p, SUB, stride=2 * SUB), :] = im[p] * scale
        out_ref[pl.ds(1 + base, SUB)] = w_ref[...].reshape(SUB, 2 * SUB, LANES).astype(jnp.bfloat16)
        return 0

    lax.fori_loop(0, stations, second, 0)
    row_ref[...] = jnp.zeros_like(row_ref)
    row_ref[0:stations, 0:SUB] = mask_ref[0].astype(jnp.float32)
    out_ref[0] = row_ref[...].astype(jnp.bfloat16)


CHUNKS = 4


def correlate_kernel(n, windows, stations, slots, pair_ref, decay_ref, own_ref, table_ref, out_ref, *scratch):
    bufs = scratch[:CHUNKS]
    (loc_ref, cr_ref, ci_ref, inv_ref, lag_ref, send_ref, got_ref, mine_ref, rate_ref, full_ref, rail_send, rail_recv,
     mate_send, mate_recv, lag_send, lag_recv, rate_send, rate_recv) = scratch[CHUNKS:]
    me, window = lax.axis_index("sta"), lax.axis_index("section")
    length = n // 2
    core, place = lax.rem(me, 2), me // 2
    mate = place * 2 + 1 - core
    segments = SUB
    wide = stations // CHUNKS
    pairs = stations * slots
    mine_ref[...] = jnp.full(mine_ref.shape, decay_ref[0], jnp.float32)

    barrier = pltpu.get_barrier_semaphore()
    has_right, has_left = place < length - 1, place > 0

    def greet(peer):
        pl.semaphore_signal(barrier, inc=1, device_id=peer, device_id_type=MESH)

    greet({"sta": mate})
    for d in range(1, windows):
        greet({"section": lax.rem(window + d, windows)})

    @pl.when(has_right)
    def _():
        greet({"sta": me + 2})

    @pl.when(has_left)
    def _():
        greet({"sta": me - 2})

    pl.semaphore_wait(barrier, windows + jnp.where(has_right, 1, 0) + jnp.where(has_left, 1, 0))

    def span(c):
        return pl.ds(0 if c == 0 else 1 + c * wide * segments, wide * segments + (1 if c == 0 else 0))

    def rail(c, d, way):
        origin = me - 2 * way * d
        src = own_ref.at[span(c)] if d == 0 else bufs[c].at[origin]
        at = (c * length + d) * 2 + (1 + way) // 2
        return pltpu.make_async_remote_copy(
            src_ref=src, dst_ref=bufs[c].at[origin], send_sem=rail_send.at[at], recv_sem=rail_recv.at[at],
            device_id={"sta": me + 2 * way}, device_id_type=MESH)

    def landed(c, d, way):
        origin = me - 2 * way * d
        at = (c * length + d - 1) * 2 + (1 + way) // 2
        return pltpu.make_async_remote_copy(
            src_ref=bufs[c].at[origin], dst_ref=bufs[c].at[origin], send_sem=rail_send.at[at],
            recv_sem=rail_recv.at[at], device_id={"sta": me + 2 * way}, device_id_type=MESH)

    def across(c, origin_place, sender_core):
        origin = origin_place * 2 + sender_core
        at = c * length + origin_place
        return pltpu.make_async_remote_copy(
            src_ref=bufs[c].at[origin], dst_ref=bufs[c].at[origin], send_sem=mate_send.at[at],
            recv_sem=mate_recv.at[at], device_id={"sta": mate}, device_id_type=MESH)

    def own_across(c):
        at = c * length + place
        return pltpu.make_async_remote_copy(
            src_ref=own_ref.at[span(c)], dst_ref=bufs[c].at[me], send_sem=mate_send.at[at],
            recv_sem=mate_recv.at[at], device_id={"sta": mate}, device_id_type=MESH)

    def onward(way, d):
        return (place - way * d >= 0) & (place - way * d < length) & (place + way >= 0) & (place + way < length)

    def holds(way, d):
        return (place - way * d >= 0) & (place - way * d < length)

    def send_own(c):
        for way in (1, -1):
            @pl.when(onward(way, 0))
            def _():
                rail(c, 0, way).start()
        own_across(c).start()

    def later(c, d):
        return (
            pltpu.make_async_remote_copy(
                src_ref=send_ref.at[c], dst_ref=got_ref.at[window, c], send_sem=lag_send.at[d * CHUNKS + c],
                recv_sem=lag_recv.at[window * CHUNKS + c], device_id={"section": window + d}, device_id_type=MESH))

    def earlier(c, v):
        return pltpu.make_async_remote_copy(
            src_ref=send_ref.at[c], dst_ref=got_ref.at[v, c], send_sem=lag_send.at[c],
            recv_sem=lag_recv.at[v * CHUNKS + c], device_id={"section": v}, device_id_type=MESH)

    def rate_later(d):
        return pltpu.make_async_remote_copy(
            src_ref=mine_ref, dst_ref=rate_ref.at[window], send_sem=rate_send.at[d],
            recv_sem=rate_recv.at[window], device_id={"section": window + d}, device_id_type=MESH)

    def rate_earlier(v):
        return pltpu.make_async_remote_copy(
            src_ref=mine_ref, dst_ref=rate_ref.at[v], send_sem=rate_send.at[0],
            recv_sem=rate_recv.at[v], device_id={"section": v}, device_id_type=MESH)

    ahead = 2
    for c in range(min(ahead, CHUNKS)):
        send_own(c)
    for d in range(1, windows):
        @pl.when(window + d < windows)
        def _():
            rate_later(d).start()
    for c in range(CHUNKS):
        bufs[c][me] = own_ref[span(c)]
    loc_ref[...] = own_ref[1:1 + stations * segments].astype(jnp.float32)

    def combine(c):
        rows = wide * pairs
        full_ref[...] = jnp.zeros_like(full_ref)
        for v in range(windows - 1):
            @pl.when(v < window)
            def _():
                if c == 0:
                    rate_earlier(v).wait_recv()
                earlier(c, v).wait_recv()
                full_ref[...] = full_ref[...] * rate_ref[v, 0:1, 0:1] + got_ref[v, c].astype(jnp.float32)
        total = full_ref[...] * mine_ref[0:1, 0:1] + lag_ref[c * rows:(c + 1) * rows, :]
        for jj in range(wide):
            for part in range(LAGS // LANES):
                cols = slice(part * LANES, (part + 1) * LANES)
                inv_ref[1 + part, pl.ds(c * wide + jj, pairs, stride=stations), :] = total[jj * pairs:(jj + 1) * pairs, cols]

    for c in range(CHUNKS):
        for d in range(1, length):
            for way in (1, -1):
                @pl.when(holds(way, d))
                def _():
                    landed(c, d, way).wait_recv()
                    across(c, place - way * d, core).start()

                @pl.when(onward(way, d))
                def _():
                    rail(c, d, way).start()
            if d == 1 and c + ahead < CHUNKS:
                send_own(c + ahead)
        for origin in range(length):
            across(c, origin, 1 - core).wait_recv()
        first = 1 if c == 0 else 0
        if c == 0:
            mine = own_ref[0].astype(jnp.float32)
            for k in range(slots):
                theirs = bufs[0][pair_ref[0, k], 0].astype(jnp.float32)[0:stations]
                for i in range(stations):
                    count = jnp.sum(mine[i:i + 1] * theirs, axis=1, keepdims=True)
                    at = (i * slots + k) * stations
                    inv_ref[0, at:at + stations, :] = jnp.broadcast_to(1.0 / jnp.maximum(count, 1.0), (stations, LANES))

        def pair(t, _):
            k, jj = t // wide, lax.rem(t, wide)
            block = pair_ref[0, k]
            other = [bufs[c][block, first + jj * segments + s].astype(jnp.float32) for s in range(segments)]
            for i in range(stations):
                re = im = None
                for s in range(segments):
                    ar, ai = loc_ref[i * segments + s, 0:SUB, :], loc_ref[i * segments + s, SUB:2 * SUB, :]
                    br, bi = other[s][0:SUB], other[s][SUB:2 * SUB]
                    tr, ti = ar * br + ai * bi, ar * bi - ai * br
                    re, im = (tr, ti) if re is None else (re + tr, im + ti)
                at = pl.ds(pl.multiple_of((jj * pairs + i * slots + k) * SUB, SUB), SUB)
                cr_ref[at, :] = re
                ci_ref[at, :] = im
            return 0

        lax.fori_loop(0, slots * wide, pair, 0)
        rows = wide * pairs
        acc = None
        for p in range(SUB):
            at = pl.ds(p, rows, stride=SUB)
            lhs = jnp.concatenate([cr_ref[at, :], ci_ref[at, :]], axis=1).astype(jnp.bfloat16)
            term = jnp.dot(lhs, table_ref[p], preferred_element_type=jnp.float32)
            acc = term if acc is None else acc + term
        for jj in range(wide):
            inv = inv_ref[0, pl.ds(c * wide + jj, pairs, stride=stations), :]
            value = acc[jj * pairs:(jj + 1) * pairs] * jnp.concatenate([inv] * (LAGS // LANES), axis=1)
            lag_ref[c * rows + jj * pairs:c * rows + (jj + 1) * pairs, :] = value
            send_ref[c, jj * pairs:(jj + 1) * pairs, :] = value.astype(jnp.bfloat16)
        for d in range(1, windows):
            @pl.when(window + d < windows)
            def _():
                later(c, d).start()
        if c > 0:
            combine(c - 1)
    combine(CHUNKS - 1)
    for part in range(LAGS // LANES):
        out_ref[:, part * LANES:(part + 1) * LANES] = inv_ref[1 + part].astype(jnp.bfloat16)
    for c in range(CHUNKS):
        for d in range(length):
            for way in (1, -1):
                @pl.when(onward(way, d))
                def _():
                    rail(c, d, way).wait_send()
        for origin in range(length):
            across(c, origin, core).wait_send()
        for d in range(1, windows):
            @pl.when(window + d < windows)
            def _():
                later(c, d).wait_send()
    for d in range(1, windows):
        @pl.when(window + d < windows)
        def _():
            rate_later(d).wait_send()


def body(sizes, waveforms, segment_mask, pair_blocks, window_decay):
    n, windows = sizes
    stations, segments = waveforms.shape[1], waveforms.shape[2]
    slots = pair_blocks.shape[1]
    rows = stations * segments
    high, low, twist = dft_tables()
    vmem = pl.BlockSpec(memory_space=pltpu.VMEM)
    smem = pl.BlockSpec(memory_space=pltpu.SMEM)
    own = pl.pallas_call(
        functools.partial(spectrum_kernel, stations),
        name="spectrum",
        out_shape=jax.ShapeDtypeStruct((1 + rows, 2 * SUB, LANES), jnp.bfloat16),
        in_specs=[vmem] * 5,
        out_specs=vmem,
        scratch_shapes=[
            pltpu.VMEM((SUB * rows, SLICES * 2 * LANES), jnp.float32),
            pltpu.VMEM((SUB * rows, 2 * LANES), jnp.float32),
            pltpu.VMEM((SUB * 2 * SUB, LANES), jnp.float32),
            pltpu.VMEM((2 * SUB, LANES), jnp.float32),
        ],
    )(waveforms, segment_mask, jnp.asarray(high), jnp.asarray(low), jnp.asarray(twist))
    dma = pltpu.SemaphoreType.DMA
    total = stations * slots * stations
    part = total // CHUNKS
    length = n // 2
    bufs = [
        pltpu.VMEM((n, rows // CHUNKS + (1 if c == 0 else 0), 2 * SUB, LANES), jnp.bfloat16) for c in range(CHUNKS)
    ]
    stacked = pl.pallas_call(
        functools.partial(correlate_kernel, n, windows, stations, slots),
        name="correlate",
        out_shape=jax.ShapeDtypeStruct((total, LAGS), jnp.bfloat16),
        in_specs=[smem, smem, vmem, vmem],
        out_specs=vmem,
        scratch_shapes=bufs + [
            pltpu.VMEM((rows, 2 * SUB, LANES), jnp.float32),
            pltpu.VMEM((part * SUB, LANES), jnp.float32),
            pltpu.VMEM((part * SUB, LANES), jnp.float32),
            pltpu.VMEM((1 + LAGS // LANES, total, LANES), jnp.float32),
            pltpu.VMEM((total, LAGS), jnp.float32),
            pltpu.VMEM((CHUNKS, part, LAGS), jnp.bfloat16),
            pltpu.VMEM((windows, CHUNKS, part, LAGS), jnp.bfloat16),
            pltpu.VMEM((SUB, LANES), jnp.float32),
            pltpu.VMEM((windows, SUB, LANES), jnp.float32),
            pltpu.VMEM((part, LAGS), jnp.float32),
            dma((2 * CHUNKS * length,)), dma((2 * CHUNKS * length,)),
            dma((CHUNKS * length,)), dma((CHUNKS * length,)),
            dma((windows * CHUNKS,)), dma((windows * CHUNKS,)),
            dma((windows,)), dma((windows,)),
        ],
        compiler_params=pltpu.CompilerParams(collective_id=0, has_side_effects=True),
    )(pair_blocks, window_decay, own, jnp.asarray(lag_table()))
    return stacked.reshape(1, stations, slots * stations, LAGS)


def solution(mesh):
    in_specs = (
        P("section", "sta", None, None),
        P("section", "sta", None),
        P("sta", None),
        P("section"),
    )
    out_specs = P("section", "sta", None, None)
    sizes = (mesh.shape["sta"], mesh.shape["section"])
    return jax.shard_map(
        functools.partial(body, sizes), mesh=mesh, in_specs=in_specs, out_specs=out_specs, check_vma=False
    )
```

```python
import functools
import math

import jax
import jax.numpy as jnp
import numpy as np
from jax import lax
from jax.experimental import pallas as pl
from jax.experimental.pallas import tpu as pltpu
from jax.sharding import PartitionSpec as P

MESH = pl.DeviceIdType.MESH
RADIX = 64
NF = 1024
LAGS = 384
SMOOTH_HALF = 32
LANES = 128
SUB = 8
EPSILON = 1e-05
NSAMP = RADIX * RADIX
FIRST = NSAMP // LANES
SLICES = FIRST // SUB
BINS = NF // FIRST


def dft_tables():
    b = np.arange(LANES)
    m = np.arange(BINS)
    phi = 2.0 * np.pi * ((b[:, None] * (m[None, :] + 2 * RADIX // FIRST)) % LANES) / LANES
    table = np.zeros((SLICES, 2, LANES, 2, BINS, SLICES))
    for q in range(SLICES):
        table[q, 0, :, 0, :, q] = np.cos(phi)
        table[q, 1, :, 0, :, q] = np.sin(phi)
        table[q, 0, :, 1, :, q] = -np.sin(phi)
        table[q, 1, :, 1, :, q] = np.cos(phi)
    table = (table / RADIX).reshape(SLICES * 2 * LANES, 2 * BINS * SLICES).astype(np.float32)
    high = table.astype(jnp.bfloat16)
    low = (table - high.astype(np.float32)).astype(jnp.bfloat16)
    turn = 2.0 * np.pi * np.arange(FIRST)[:, None] * b[None, :] / NSAMP
    twist = np.stack([np.cos(turn), np.sin(turn)], axis=1).astype(np.float32)
    return high, low, twist


def lag_table():
    f = SUB * np.arange(NF // SUB)[None, :] + np.arange(SUB)[:, None]
    shift = np.arange(LAGS) + NSAMP - LAGS // 2
    theta = 2.0 * np.pi * (((2 * RADIX + f)[:, :, None] * shift) % NSAMP) / NSAMP
    table = np.concatenate([np.cos(theta), -np.sin(theta)], axis=1) / math.sqrt(NF)
    return table.astype(np.float32).astype(jnp.bfloat16)


def real_dft(values):
    size = len(values)
    if size == 1:
        return [(values[0], None)]
    if size == 2:
        return [(values[0] + values[1], None), (values[0] - values[1], None)]
    even, odd = real_dft(values[0::2]), real_dft(values[1::2])
    half = size // 2
    out = [None] * (half + 1)
    for k in range(half // 2 + 1):
        er, ei = even[k]
        pr, pi = odd[k]
        if k == 0:
            out[0] = (er + pr, None)
            out[half] = (er - pr, None)
            continue
        if k * 4 == size:
            out[k] = (er, -pr)
            continue
        c, s = math.cos(2 * math.pi * k / size), math.sin(2 * math.pi * k / size)
        tr, ti = pr * c + pi * s, pi * c - pr * s
        out[k] = (er + tr, ei + ti)
        out[half - k] = (er - tr, ti - ei)
    return out


def spectrum_kernel(stations, x_ref, mask_ref, high_ref, low_ref, twist_ref, out_ref, y_ref, z_ref, w_ref, row_ref):
    rows = stations * SUB

    def first(st, _):
        pieces = [x_ref[0, st, :, a * LANES:(a + 1) * LANES].astype(jnp.float32) for a in range(FIRST)]
        spread = real_dft(pieces)
        base = pl.multiple_of(st * SUB, SUB)
        for k1 in range(FIRST):
            re, im = spread[k1] if 2 * k1 <= FIRST else spread[FIRST - k1]
            c, s = twist_ref[k1, 0:1, :], twist_ref[k1, 1:2, :]
            if im is None:
                yr, yi = re * c, -(re * s)
            elif 2 * k1 <= FIRST:
                yr, yi = re * c + im * s, im * c - re * s
            else:
                yr, yi = re * c - im * s, -(im * c) - re * s
            q, p = k1 // SUB, k1 % SUB
            y_ref[pl.ds(p * rows + base, SUB), 2 * q * LANES:(2 * q + 1) * LANES] = yr
            y_ref[pl.ds(p * rows + base, SUB), (2 * q + 1) * LANES:(2 * q + 2) * LANES] = yi
        return 0

    lax.fori_loop(0, stations, first, 0)
    y = y_ref[...]
    yh = y.astype(jnp.bfloat16)
    yl = (y - yh.astype(jnp.float32)).astype(jnp.bfloat16)
    dot = functools.partial(jnp.dot, preferred_element_type=jnp.float32)
    z_ref[...] = dot(yh, high_ref[...]) + dot(yl, high_ref[...]) + dot(yh, low_ref[...])
    reach = SMOOTH_HALF // SUB
    square = lax.broadcasted_iota(jnp.int32, (SUB, SUB), 0) == lax.broadcasted_iota(jnp.int32, (SUB, SUB), 1)

    def second(st, _):
        base = pl.multiple_of(st * SUB, SUB)
        lane = lax.broadcasted_iota(jnp.int32, (SUB, LANES), 1)

        def moved(v, d):
            inside = (lane + d >= 0) & (lane + d < LANES)
            return jnp.where(inside, pltpu.roll(v, (-d) % LANES, 1), 0.0)

        re = [z_ref[pl.ds(p * rows + base, SUB), 0:LANES] for p in range(SUB)]
        im = [z_ref[pl.ds(p * rows + base, SUB), LANES:2 * LANES] for p in range(SUB)]
        amp = [jnp.sqrt(re[p] * re[p] + im[p] * im[p]) for p in range(SUB)]
        pre = [amp[0]]
        for p in range(1, SUB):
            pre.append(pre[-1] + amp[p])
        suf = [amp[SUB - 1]]
        for p in range(SUB - 2, -1, -1):
            suf.insert(0, suf[0] + amp[p])
        middle = pre[-1]
        for d in range(1, reach):
            middle = middle + moved(pre[-1], d) + moved(pre[-1], -d)
        row = jnp.broadcast_to(mask_ref[0, pl.ds(st, 1), :].astype(jnp.float32), (SUB, SUB))
        marks = jnp.sum(jnp.where(square, row, 0.0), axis=1, keepdims=True)
        for p in range(SUB):
            smooth = (middle + moved(suf[p], -reach) + moved(pre[p], reach)) / (2 * SMOOTH_HALF + 1)
            scale = marks / (smooth + EPSILON)
            w_ref[pl.ds(p, SUB, stride=2 * SUB), :] = re[p] * scale
            w_ref[pl.ds(SUB + p, SUB, stride=2 * SUB), :] = im[p] * scale
        out_ref[pl.ds(1 + base, SUB)] = w_ref[...].reshape(SUB, 2 * SUB, LANES).astype(jnp.bfloat16)
        return 0

    lax.fori_loop(0, stations, second, 0)
    row_ref[...] = jnp.zeros_like(row_ref)
    row_ref[0:stations, 0:SUB] = mask_ref[0].astype(jnp.float32)
    out_ref[0] = row_ref[...].astype(jnp.bfloat16)


CHUNKS = 4


def correlate_kernel(n, windows, stations, slots, pair_ref, decay_ref, own_ref, table_ref, out_ref, *scratch):
    bufs = scratch[:CHUNKS]
    (loc_ref, cr_ref, ci_ref, inv_ref, lag_ref, send_ref, got_ref, mine_ref, rate_ref, full_ref, rail_send, rail_recv,
     mate_send, mate_recv, lag_send, lag_recv, rate_send, rate_recv) = scratch[CHUNKS:]
    me, window = lax.axis_index("sta"), lax.axis_index("section")
    length = n // 2
    core, place = lax.rem(me, 2), me // 2
    mate = place * 2 + 1 - core
    segments = SUB
    wide = stations // CHUNKS
    pairs = stations * slots
    mine_ref[...] = jnp.full(mine_ref.shape, decay_ref[0], jnp.float32)

    barrier = pltpu.get_barrier_semaphore()
    has_right, has_left = place < length - 1, place > 0

    def greet(peer):
        pl.semaphore_signal(barrier, inc=1, device_id=peer, device_id_type=MESH)

    greet({"sta": mate})
    for d in range(1, windows):
        greet({"section": lax.rem(window + d, windows)})

    @pl.when(has_right)
    def _():
        greet({"sta": me + 2})

    @pl.when(has_left)
    def _():
        greet({"sta": me - 2})

    pl.semaphore_wait(barrier, windows + jnp.where(has_right, 1, 0) + jnp.where(has_left, 1, 0))

    def span(c):
        return pl.ds(0 if c == 0 else 1 + c * wide * segments, wide * segments + (1 if c == 0 else 0))

    def rail(c, d, way):
        origin = me - 2 * way * d
        src = own_ref.at[span(c)] if d == 0 else bufs[c].at[origin]
        at = (c * length + d) * 2 + (1 + way) // 2
        return pltpu.make_async_remote_copy(
            src_ref=src, dst_ref=bufs[c].at[origin], send_sem=rail_send.at[at], recv_sem=rail_recv.at[at],
            device_id={"sta": me + 2 * way}, device_id_type=MESH)

    def landed(c, d, way):
        origin = me - 2 * way * d
        at = (c * length + d - 1) * 2 + (1 + way) // 2
        return pltpu.make_async_remote_copy(
            src_ref=bufs[c].at[origin], dst_ref=bufs[c].at[origin], send_sem=rail_send.at[at],
            recv_sem=rail_recv.at[at], device_id={"sta": me + 2 * way}, device_id_type=MESH)

    def across(c, origin_place, sender_core):
        origin = origin_place * 2 + sender_core
        at = c * length + origin_place
        return pltpu.make_async_remote_copy(
            src_ref=bufs[c].at[origin], dst_ref=bufs[c].at[origin], send_sem=mate_send.at[at],
            recv_sem=mate_recv.at[at], device_id={"sta": mate}, device_id_type=MESH)

    def own_across(c):
        at = c * length + place
        return pltpu.make_async_remote_copy(
            src_ref=own_ref.at[span(c)], dst_ref=bufs[c].at[me], send_sem=mate_send.at[at],
            recv_sem=mate_recv.at[at], device_id={"sta": mate}, device_id_type=MESH)

    def onward(way, d):
        return (place - way * d >= 0) & (place - way * d < length) & (place + way >= 0) & (place + way < length)

    def holds(way, d):
        return (place - way * d >= 0) & (place - way * d < length)

    def send_own(c):
        for way in (1, -1):
            @pl.when(onward(way, 0))
            def _():
                rail(c, 0, way).start()
        own_across(c).start()

    def later(c, d):
        return (
            pltpu.make_async_remote_copy(
                src_ref=send_ref.at[c], dst_ref=got_ref.at[window, c], send_sem=lag_send.at[d * CHUNKS + c],
                recv_sem=lag_recv.at[window * CHUNKS + c], device_id={"section": window + d}, device_id_type=MESH))

    def earlier(c, v):
        return pltpu.make_async_remote_copy(
            src_ref=send_ref.at[c], dst_ref=got_ref.at[v, c], send_sem=lag_send.at[c],
            recv_sem=lag_recv.at[v * CHUNKS + c], device_id={"section": v}, device_id_type=MESH)

    def rate_later(d):
        return pltpu.make_async_remote_copy(
            src_ref=mine_ref, dst_ref=rate_ref.at[window], send_sem=rate_send.at[d],
            recv_sem=rate_recv.at[window], device_id={"section": window + d}, device_id_type=MESH)

    def rate_earlier(v):
        return pltpu.make_async_remote_copy(
            src_ref=mine_ref, dst_ref=rate_ref.at[v], send_sem=rate_send.at[0],
            recv_sem=rate_recv.at[v], device_id={"section": v}, device_id_type=MESH)

    ahead = 2
    for c in range(min(ahead, CHUNKS)):
        send_own(c)
    for d in range(1, windows):
        @pl.when(window + d < windows)
        def _():
            rate_later(d).start()
    for c in range(CHUNKS):
        bufs[c][me] = own_ref[span(c)]
    loc_ref[...] = own_ref[1:1 + stations * segments].astype(jnp.float32)

    def combine(c):
        rows = wide * pairs
        full_ref[...] = jnp.zeros_like(full_ref)
        for v in range(windows - 1):
            @pl.when(v < window)
            def _():
                if c == 0:
                    rate_earlier(v).wait_recv()
                earlier(c, v).wait_recv()
                full_ref[...] = full_ref[...] * rate_ref[v, 0:1, 0:1] + got_ref[v, c].astype(jnp.float32)
        total = full_ref[...] * mine_ref[0:1, 0:1] + lag_ref[c * rows:(c + 1) * rows, :]
        for jj in range(wide):
            for part in range(LAGS // LANES):
                cols = slice(part * LANES, (part + 1) * LANES)
                inv_ref[1 + part, pl.ds(c * wide + jj, pairs, stride=stations), :] = total[jj * pairs:(jj + 1) * pairs, cols]

    def relay(c):
        for d in range(1, length):
            for way in (1, -1):
                @pl.when(holds(way, d))
                def _():
                    landed(c, d, way).wait_recv()

                @pl.when(onward(way, d))
                def _():
                    rail(c, d, way).start()

                @pl.when(holds(way, d))
                def _():
                    across(c, place - way * d, core).start()
            if d == 1 and c + ahead < CHUNKS:
                send_own(c + ahead)

    relay(0)
    for c in range(CHUNKS):
        if c + 1 < CHUNKS:
            relay(c + 1)
        for origin in range(length):
            across(c, origin, 1 - core).wait_recv()
        first = 1 if c == 0 else 0
        if c == 0:
            mine = own_ref[0].astype(jnp.float32)
            for k in range(slots):
                theirs = bufs[0][pair_ref[0, k], 0].astype(jnp.float32)[0:stations]
                for i in range(stations):
                    count = jnp.sum(mine[i:i + 1] * theirs, axis=1, keepdims=True)
                    at = (i * slots + k) * stations
                    inv_ref[0, at:at + stations, :] = jnp.broadcast_to(1.0 / jnp.maximum(count, 1.0), (stations, LANES))

        def pair(t, _):
            k, jj = t // wide, lax.rem(t, wide)
            block = pair_ref[0, k]
            other = [bufs[c][block, first + jj * segments + s].astype(jnp.float32) for s in range(segments)]
            for i in range(stations):
                re = im = None
                for s in range(segments):
                    ar, ai = loc_ref[i * segments + s, 0:SUB, :], loc_ref[i * segments + s, SUB:2 * SUB, :]
                    br, bi = other[s][0:SUB], other[s][SUB:2 * SUB]
                    tr, ti = ar * br + ai * bi, ar * bi - ai * br
                    re, im = (tr, ti) if re is None else (re + tr, im + ti)
                at = pl.ds(pl.multiple_of((jj * pairs + i * slots + k) * SUB, SUB), SUB)
                cr_ref[at, :] = re
                ci_ref[at, :] = im
            return 0

        lax.fori_loop(0, slots * wide, pair, 0)
        rows = wide * pairs
        acc = None
        for p in range(SUB):
            at = pl.ds(p, rows, stride=SUB)
            lhs = jnp.concatenate([cr_ref[at, :], ci_ref[at, :]], axis=1).astype(jnp.bfloat16)
            term = jnp.dot(lhs, table_ref[p], preferred_element_type=jnp.float32)
            acc = term if acc is None else acc + term
        for jj in range(wide):
            inv = inv_ref[0, pl.ds(c * wide + jj, pairs, stride=stations), :]
            value = acc[jj * pairs:(jj + 1) * pairs] * jnp.concatenate([inv] * (LAGS // LANES), axis=1)
            lag_ref[c * rows + jj * pairs:c * rows + (jj + 1) * pairs, :] = value
            send_ref[c, jj * pairs:(jj + 1) * pairs, :] = value.astype(jnp.bfloat16)
        for d in range(1, windows):
            @pl.when(window + d < windows)
            def _():
                later(c, d).start()
        if c > 0:
            combine(c - 1)
    combine(CHUNKS - 1)
    for part in range(LAGS // LANES):
        out_ref[:, part * LANES:(part + 1) * LANES] = inv_ref[1 + part].astype(jnp.bfloat16)
    for c in range(CHUNKS):
        for d in range(length):
            for way in (1, -1):
                @pl.when(onward(way, d))
                def _():
                    rail(c, d, way).wait_send()
        for origin in range(length):
            across(c, origin, core).wait_send()
        for d in range(1, windows):
            @pl.when(window + d < windows)
            def _():
                later(c, d).wait_send()
    for d in range(1, windows):
        @pl.when(window + d < windows)
        def _():
            rate_later(d).wait_send()


def body(sizes, waveforms, segment_mask, pair_blocks, window_decay):
    n, windows = sizes
    stations, segments = waveforms.shape[1], waveforms.shape[2]
    slots = pair_blocks.shape[1]
    rows = stations * segments
    high, low, twist = dft_tables()
    vmem = pl.BlockSpec(memory_space=pltpu.VMEM)
    smem = pl.BlockSpec(memory_space=pltpu.SMEM)
    own = pl.pallas_call(
        functools.partial(spectrum_kernel, stations),
        name="spectrum",
        out_shape=jax.ShapeDtypeStruct((1 + rows, 2 * SUB, LANES), jnp.bfloat16),
        in_specs=[vmem] * 5,
        out_specs=vmem,
        scratch_shapes=[
            pltpu.VMEM((SUB * rows, SLICES * 2 * LANES), jnp.float32),
            pltpu.VMEM((SUB * rows, 2 * LANES), jnp.float32),
            pltpu.VMEM((SUB * 2 * SUB, LANES), jnp.float32),
            pltpu.VMEM((2 * SUB, LANES), jnp.float32),
        ],
    )(waveforms, segment_mask, jnp.asarray(high), jnp.asarray(low), jnp.asarray(twist))
    dma = pltpu.SemaphoreType.DMA
    total = stations * slots * stations
    part = total // CHUNKS
    length = n // 2
    bufs = [
        pltpu.VMEM((n, rows // CHUNKS + (1 if c == 0 else 0), 2 * SUB, LANES), jnp.bfloat16) for c in range(CHUNKS)
    ]
    stacked = pl.pallas_call(
        functools.partial(correlate_kernel, n, windows, stations, slots),
        name="correlate",
        out_shape=jax.ShapeDtypeStruct((total, LAGS), jnp.bfloat16),
        in_specs=[smem, smem, vmem, vmem],
        out_specs=vmem,
        scratch_shapes=bufs + [
            pltpu.VMEM((rows, 2 * SUB, LANES), jnp.float32),
            pltpu.VMEM((part * SUB, LANES), jnp.float32),
            pltpu.VMEM((part * SUB, LANES), jnp.float32),
            pltpu.VMEM((1 + LAGS // LANES, total, LANES), jnp.float32),
            pltpu.VMEM((total, LAGS), jnp.float32),
            pltpu.VMEM((CHUNKS, part, LAGS), jnp.bfloat16),
            pltpu.VMEM((windows, CHUNKS, part, LAGS), jnp.bfloat16),
            pltpu.VMEM((SUB, LANES), jnp.float32),
            pltpu.VMEM((windows, SUB, LANES), jnp.float32),
            pltpu.VMEM((part, LAGS), jnp.float32),
            dma((2 * CHUNKS * length,)), dma((2 * CHUNKS * length,)),
            dma((CHUNKS * length,)), dma((CHUNKS * length,)),
            dma((windows * CHUNKS,)), dma((windows * CHUNKS,)),
            dma((windows,)), dma((windows,)),
        ],
        compiler_params=pltpu.CompilerParams(collective_id=0, has_side_effects=True),
    )(pair_blocks, window_decay, own, jnp.asarray(lag_table()))
    return stacked.reshape(1, stations, slots * stations, LAGS)


def solution(mesh):
    in_specs = (
        P("section", "sta", None, None),
        P("section", "sta", None),
        P("sta", None),
        P("section"),
    )
    out_specs = P("section", "sta", None, None)
    sizes = (mesh.shape["sta"], mesh.shape["section"])
    return jax.shard_map(
        functools.partial(body, sizes), mesh=mesh, in_specs=in_specs, out_specs=out_specs, check_vma=False
    )
```

```python
import functools
import math

import jax
import jax.numpy as jnp
import numpy as np
from jax import lax
from jax.experimental import pallas as pl
from jax.experimental.pallas import tpu as pltpu
from jax.sharding import PartitionSpec as P

MESH = pl.DeviceIdType.MESH
RADIX = 64
NF = 1024
LAGS = 384
SMOOTH_HALF = 32
LANES = 128
SUB = 8
EPSILON = 1e-05
NSAMP = RADIX * RADIX
FIRST = NSAMP // LANES
SLICES = FIRST // SUB
BINS = NF // FIRST


def dft_tables():
    b = np.arange(LANES)
    m = np.arange(BINS)
    phi = 2.0 * np.pi * ((b[:, None] * (m[None, :] + 2 * RADIX // FIRST)) % LANES) / LANES
    table = np.zeros((SLICES, 2, LANES, 2, BINS, SLICES))
    for q in range(SLICES):
        table[q, 0, :, 0, :, q] = np.cos(phi)
        table[q, 1, :, 0, :, q] = np.sin(phi)
        table[q, 0, :, 1, :, q] = -np.sin(phi)
        table[q, 1, :, 1, :, q] = np.cos(phi)
    table = (table / RADIX).reshape(SLICES * 2 * LANES, 2 * BINS * SLICES).astype(np.float32)
    high = table.astype(jnp.bfloat16)
    low = (table - high.astype(np.float32)).astype(jnp.bfloat16)
    turn = 2.0 * np.pi * np.arange(FIRST)[:, None] * b[None, :] / NSAMP
    twist = np.stack([np.cos(turn), np.sin(turn)], axis=1).astype(np.float32)
    return high, low, twist


def lag_table():
    f = SUB * np.arange(NF // SUB)[None, :] + np.arange(SUB)[:, None]
    shift = np.arange(LAGS) + NSAMP - LAGS // 2
    theta = 2.0 * np.pi * (((2 * RADIX + f)[:, :, None] * shift) % NSAMP) / NSAMP
    table = np.concatenate([np.cos(theta), -np.sin(theta)], axis=1) / math.sqrt(NF)
    return table.astype(np.float32).astype(jnp.bfloat16)


def real_dft(values):
    size = len(values)
    if size == 1:
        return [(values[0], None)]
    if size == 2:
        return [(values[0] + values[1], None), (values[0] - values[1], None)]
    even, odd = real_dft(values[0::2]), real_dft(values[1::2])
    half = size // 2
    out = [None] * (half + 1)
    for k in range(half // 2 + 1):
        er, ei = even[k]
        pr, pi = odd[k]
        if k == 0:
            out[0] = (er + pr, None)
            out[half] = (er - pr, None)
            continue
        if k * 4 == size:
            out[k] = (er, -pr)
            continue
        c, s = math.cos(2 * math.pi * k / size), math.sin(2 * math.pi * k / size)
        tr, ti = pr * c + pi * s, pi * c - pr * s
        out[k] = (er + tr, ei + ti)
        out[half - k] = (er - tr, ti - ei)
    return out


def spectrum(begin, count, x_ref, mask_ref, high_ref, low_ref, twist_ref, out_ref, y_ref, z_ref, w_ref):
    rows = count * SUB

    def first(st, _):
        pieces = [x_ref[0, begin + st, :, a * LANES:(a + 1) * LANES].astype(jnp.float32) for a in range(FIRST)]
        spread = real_dft(pieces)
        base = pl.multiple_of(st * SUB, SUB)
        for k1 in range(FIRST):
            re, im = spread[k1] if 2 * k1 <= FIRST else spread[FIRST - k1]
            c, s = twist_ref[k1, 0:1, :], twist_ref[k1, 1:2, :]
            if im is None:
                yr, yi = re * c, -(re * s)
            elif 2 * k1 <= FIRST:
                yr, yi = re * c + im * s, im * c - re * s
            else:
                yr, yi = re * c - im * s, -(im * c) - re * s
            q, p = k1 // SUB, k1 % SUB
            y_ref[pl.ds(p * rows + base, SUB), 2 * q * LANES:(2 * q + 1) * LANES] = yr
            y_ref[pl.ds(p * rows + base, SUB), (2 * q + 1) * LANES:(2 * q + 2) * LANES] = yi
        return 0

    lax.fori_loop(0, count, first, 0)
    y = y_ref[...]
    yh = y.astype(jnp.bfloat16)
    yl = (y - yh.astype(jnp.float32)).astype(jnp.bfloat16)
    dot = functools.partial(jnp.dot, preferred_element_type=jnp.float32)
    z_ref[...] = dot(yh, high_ref[...]) + dot(yl, high_ref[...]) + dot(yh, low_ref[...])
    reach = SMOOTH_HALF // SUB
    square = lax.broadcasted_iota(jnp.int32, (SUB, SUB), 0) == lax.broadcasted_iota(jnp.int32, (SUB, SUB), 1)

    def second(st, _):
        base = pl.multiple_of(st * SUB, SUB)
        lane = lax.broadcasted_iota(jnp.int32, (SUB, LANES), 1)

        def moved(v, d):
            inside = (lane + d >= 0) & (lane + d < LANES)
            return jnp.where(inside, pltpu.roll(v, (-d) % LANES, 1), 0.0)

        re = [z_ref[pl.ds(p * rows + base, SUB), 0:LANES] for p in range(SUB)]
        im = [z_ref[pl.ds(p * rows + base, SUB), LANES:2 * LANES] for p in range(SUB)]
        amp = [jnp.sqrt(re[p] * re[p] + im[p] * im[p]) for p in range(SUB)]
        pre = [amp[0]]
        for p in range(1, SUB):
            pre.append(pre[-1] + amp[p])
        suf = [amp[SUB - 1]]
        for p in range(SUB - 2, -1, -1):
            suf.insert(0, suf[0] + amp[p])
        middle = pre[-1]
        for d in range(1, reach):
            middle = middle + moved(pre[-1], d) + moved(pre[-1], -d)
        row = jnp.broadcast_to(mask_ref[0, pl.ds(begin + st, 1), :].astype(jnp.float32), (SUB, SUB))
        marks = jnp.sum(jnp.where(square, row, 0.0), axis=1, keepdims=True)
        for p in range(SUB):
            smooth = (middle + moved(suf[p], -reach) + moved(pre[p], reach)) / (2 * SMOOTH_HALF + 1)
            scale = marks / (smooth + EPSILON)
            w_ref[pl.ds(p, SUB, stride=2 * SUB), :] = re[p] * scale
            w_ref[pl.ds(SUB + p, SUB, stride=2 * SUB), :] = im[p] * scale
        out_ref[pl.ds(1 + begin * SUB + base, SUB)] = w_ref[...].reshape(SUB, 2 * SUB, LANES).astype(jnp.bfloat16)
        return 0

    lax.fori_loop(0, count, second, 0)


CHUNKS = 4


def correlate_kernel(n, windows, stations, slots, pair_ref, decay_ref, x_ref, mask_ref, high_ref,
                     low_ref, twist_ref, table_ref, out_ref, *scratch):
    bufs = scratch[:CHUNKS]
    (loc_ref, cr_ref, ci_ref, inv_ref, lag_ref, send_ref, got_ref, mine_ref, rate_ref, full_ref, rail_send, rail_recv,
     mate_send, mate_recv, lag_send, lag_recv, rate_send, rate_recv, own_ref, y_ref, z_ref, w_ref, row_ref) = scratch[CHUNKS:]
    me, window = lax.axis_index("sta"), lax.axis_index("section")
    length = n // 2
    core, place = lax.rem(me, 2), me // 2
    mate = place * 2 + 1 - core
    segments = SUB
    wide = stations // CHUNKS
    pairs = stations * slots
    mine_ref[...] = jnp.full(mine_ref.shape, decay_ref[0], jnp.float32)

    barrier = pltpu.get_barrier_semaphore()
    has_right, has_left = place < length - 1, place > 0

    def greet(peer):
        pl.semaphore_signal(barrier, inc=1, device_id=peer, device_id_type=MESH)

    greet({"sta": mate})
    for d in range(1, windows):
        greet({"section": lax.rem(window + d, windows)})

    @pl.when(has_right)
    def _():
        greet({"sta": me + 2})

    @pl.when(has_left)
    def _():
        greet({"sta": me - 2})

    def transform(c):
        spectrum(c * wide, wide, x_ref, mask_ref, high_ref, low_ref, twist_ref, own_ref, y_ref, z_ref, w_ref)

    row_ref[...] = jnp.zeros_like(row_ref)
    row_ref[0:stations, 0:SUB] = mask_ref[0].astype(jnp.float32)
    own_ref[0] = row_ref[...].astype(jnp.bfloat16)
    transform(0)
    pl.semaphore_wait(barrier, windows + jnp.where(has_right, 1, 0) + jnp.where(has_left, 1, 0))

    def span(c):
        return pl.ds(0 if c == 0 else 1 + c * wide * segments, wide * segments + (1 if c == 0 else 0))

    def rail(c, d, way):
        origin = me - 2 * way * d
        src = own_ref.at[span(c)] if d == 0 else bufs[c].at[origin]
        at = (c * length + d) * 2 + (1 + way) // 2
        return pltpu.make_async_remote_copy(
            src_ref=src, dst_ref=bufs[c].at[origin], send_sem=rail_send.at[at], recv_sem=rail_recv.at[at],
            device_id={"sta": me + 2 * way}, device_id_type=MESH)

    def landed(c, d, way):
        origin = me - 2 * way * d
        at = (c * length + d - 1) * 2 + (1 + way) // 2
        return pltpu.make_async_remote_copy(
            src_ref=bufs[c].at[origin], dst_ref=bufs[c].at[origin], send_sem=rail_send.at[at],
            recv_sem=rail_recv.at[at], device_id={"sta": me + 2 * way}, device_id_type=MESH)

    def across(c, origin_place, sender_core):
        origin = origin_place * 2 + sender_core
        at = c * length + origin_place
        return pltpu.make_async_remote_copy(
            src_ref=bufs[c].at[origin], dst_ref=bufs[c].at[origin], send_sem=mate_send.at[at],
            recv_sem=mate_recv.at[at], device_id={"sta": mate}, device_id_type=MESH)

    def own_across(c):
        at = c * length + place
        return pltpu.make_async_remote_copy(
            src_ref=own_ref.at[span(c)], dst_ref=bufs[c].at[me], send_sem=mate_send.at[at],
            recv_sem=mate_recv.at[at], device_id={"sta": mate}, device_id_type=MESH)

    def onward(way, d):
        return (place - way * d >= 0) & (place - way * d < length) & (place + way >= 0) & (place + way < length)

    def holds(way, d):
        return (place - way * d >= 0) & (place - way * d < length)

    def send_own(c):
        for way in (1, -1):
            @pl.when(onward(way, 0))
            def _():
                rail(c, 0, way).start()
        own_across(c).start()

    def later(c, d):
        return (
            pltpu.make_async_remote_copy(
                src_ref=send_ref.at[c], dst_ref=got_ref.at[window, c], send_sem=lag_send.at[d * CHUNKS + c],
                recv_sem=lag_recv.at[window * CHUNKS + c], device_id={"section": window + d}, device_id_type=MESH))

    def earlier(c, v):
        return pltpu.make_async_remote_copy(
            src_ref=send_ref.at[c], dst_ref=got_ref.at[v, c], send_sem=lag_send.at[c],
            recv_sem=lag_recv.at[v * CHUNKS + c], device_id={"section": v}, device_id_type=MESH)

    def rate_later(d):
        return pltpu.make_async_remote_copy(
            src_ref=mine_ref, dst_ref=rate_ref.at[window], send_sem=rate_send.at[d],
            recv_sem=rate_recv.at[window], device_id={"section": window + d}, device_id_type=MESH)

    def rate_earlier(v):
        return pltpu.make_async_remote_copy(
            src_ref=mine_ref, dst_ref=rate_ref.at[v], send_sem=rate_send.at[0],
            recv_sem=rate_recv.at[v], device_id={"section": v}, device_id_type=MESH)

    ahead = 2
    send_own(0)
    for d in range(1, windows):
        @pl.when(window + d < windows)
        def _():
            rate_later(d).start()
    for c in range(1, CHUNKS):
        transform(c)
        if 1 <= c - 1 < ahead:
            send_own(c - 1)
    for c in range(CHUNKS):
        bufs[c][me] = own_ref[span(c)]
    loc_ref[...] = own_ref[1:1 + stations * segments].astype(jnp.float32)

    def combine(c):
        rows = wide * pairs
        full_ref[...] = jnp.zeros_like(full_ref)
        for v in range(windows - 1):
            @pl.when(v < window)
            def _():
                if c == 0:
                    rate_earlier(v).wait_recv()
                earlier(c, v).wait_recv()
                full_ref[...] = full_ref[...] * rate_ref[v, 0:1, 0:1] + got_ref[v, c].astype(jnp.float32)
        total = full_ref[...] * mine_ref[0:1, 0:1] + lag_ref[c * rows:(c + 1) * rows, :]
        for jj in range(wide):
            for part in range(LAGS // LANES):
                cols = slice(part * LANES, (part + 1) * LANES)
                inv_ref[1 + part, pl.ds(c * wide + jj, pairs, stride=stations), :] = total[jj * pairs:(jj + 1) * pairs, cols]

    def relay(c):
        for d in range(1, length):
            for way in (1, -1):
                @pl.when(holds(way, d))
                def _():
                    landed(c, d, way).wait_recv()

                @pl.when(onward(way, d))
                def _():
                    rail(c, d, way).start()

                @pl.when(holds(way, d))
                def _():
                    across(c, place - way * d, core).start()
            if d == 1 and c + ahead < CHUNKS:
                send_own(c + ahead)

    relay(0)
    for c in range(CHUNKS):
        if c + 1 < CHUNKS:
            relay(c + 1)
        for origin in range(length):
            across(c, origin, 1 - core).wait_recv()
        first = 1 if c == 0 else 0
        if c == 0:
            mine = own_ref[0].astype(jnp.float32)
            for k in range(slots):
                theirs = bufs[0][pair_ref[0, k], 0].astype(jnp.float32)[0:stations]
                for i in range(stations):
                    count = jnp.sum(mine[i:i + 1] * theirs, axis=1, keepdims=True)
                    at = (i * slots + k) * stations
                    inv_ref[0, at:at + stations, :] = jnp.broadcast_to(1.0 / jnp.maximum(count, 1.0), (stations, LANES))

        def pair(t, _):
            k, jj = t // wide, lax.rem(t, wide)
            block = pair_ref[0, k]
            other = [bufs[c][block, first + jj * segments + s].astype(jnp.float32) for s in range(segments)]
            for i in range(stations):
                re = im = None
                for s in range(segments):
                    ar, ai = loc_ref[i * segments + s, 0:SUB, :], loc_ref[i * segments + s, SUB:2 * SUB, :]
                    br, bi = other[s][0:SUB], other[s][SUB:2 * SUB]
                    tr, ti = ar * br + ai * bi, ar * bi - ai * br
                    re, im = (tr, ti) if re is None else (re + tr, im + ti)
                at = pl.ds(pl.multiple_of((jj * pairs + i * slots + k) * SUB, SUB), SUB)
                cr_ref[at, :] = re
                ci_ref[at, :] = im
            return 0

        lax.fori_loop(0, slots * wide, pair, 0)
        rows = wide * pairs
        acc = None
        for p in range(SUB):
            at = pl.ds(p, rows, stride=SUB)
            lhs = jnp.concatenate([cr_ref[at, :], ci_ref[at, :]], axis=1).astype(jnp.bfloat16)
            term = jnp.dot(lhs, table_ref[p], preferred_element_type=jnp.float32)
            acc = term if acc is None else acc + term
        for jj in range(wide):
            inv = inv_ref[0, pl.ds(c * wide + jj, pairs, stride=stations), :]
            value = acc[jj * pairs:(jj + 1) * pairs] * jnp.concatenate([inv] * (LAGS // LANES), axis=1)
            lag_ref[c * rows + jj * pairs:c * rows + (jj + 1) * pairs, :] = value
            send_ref[c, jj * pairs:(jj + 1) * pairs, :] = value.astype(jnp.bfloat16)
        for d in range(1, windows):
            @pl.when(window + d < windows)
            def _():
                later(c, d).start()
        if c > 0:
            combine(c - 1)
    combine(CHUNKS - 1)
    for part in range(LAGS // LANES):
        out_ref[:, part * LANES:(part + 1) * LANES] = inv_ref[1 + part].astype(jnp.bfloat16)
    for c in range(CHUNKS):
        for d in range(length):
            for way in (1, -1):
                @pl.when(onward(way, d))
                def _():
                    rail(c, d, way).wait_send()
        for origin in range(length):
            across(c, origin, core).wait_send()
        for d in range(1, windows):
            @pl.when(window + d < windows)
            def _():
                later(c, d).wait_send()
    for d in range(1, windows):
        @pl.when(window + d < windows)
        def _():
            rate_later(d).wait_send()


def body(sizes, waveforms, segment_mask, pair_blocks, window_decay):
    n, windows = sizes
    stations, segments = waveforms.shape[1], waveforms.shape[2]
    slots = pair_blocks.shape[1]
    rows = stations * segments
    high, low, twist = dft_tables()
    vmem = pl.BlockSpec(memory_space=pltpu.VMEM)
    smem = pl.BlockSpec(memory_space=pltpu.SMEM)
    dma = pltpu.SemaphoreType.DMA
    total = stations * slots * stations
    part = total // CHUNKS
    length = n // 2
    bufs = [
        pltpu.VMEM((n, rows // CHUNKS + (1 if c == 0 else 0), 2 * SUB, LANES), jnp.bfloat16) for c in range(CHUNKS)
    ]
    stacked = pl.pallas_call(
        functools.partial(correlate_kernel, n, windows, stations, slots),
        name="correlate",
        out_shape=jax.ShapeDtypeStruct((total, LAGS), jnp.bfloat16),
        in_specs=[smem, smem] + [vmem] * 6,
        out_specs=vmem,
        scratch_shapes=bufs + [
            pltpu.VMEM((rows, 2 * SUB, LANES), jnp.float32),
            pltpu.VMEM((part * SUB, LANES), jnp.float32),
            pltpu.VMEM((part * SUB, LANES), jnp.float32),
            pltpu.VMEM((1 + LAGS // LANES, total, LANES), jnp.float32),
            pltpu.VMEM((total, LAGS), jnp.float32),
            pltpu.VMEM((CHUNKS, part, LAGS), jnp.bfloat16),
            pltpu.VMEM((windows, CHUNKS, part, LAGS), jnp.bfloat16),
            pltpu.VMEM((SUB, LANES), jnp.float32),
            pltpu.VMEM((windows, SUB, LANES), jnp.float32),
            pltpu.VMEM((part, LAGS), jnp.float32),
            dma((2 * CHUNKS * length,)), dma((2 * CHUNKS * length,)),
            dma((CHUNKS * length,)), dma((CHUNKS * length,)),
            dma((windows * CHUNKS,)), dma((windows * CHUNKS,)),
            dma((windows,)), dma((windows,)),
            pltpu.VMEM((1 + rows, 2 * SUB, LANES), jnp.bfloat16),
            pltpu.VMEM((SUB * rows // CHUNKS, SLICES * 2 * LANES), jnp.float32),
            pltpu.VMEM((SUB * rows // CHUNKS, 2 * LANES), jnp.float32),
            pltpu.VMEM((SUB * 2 * SUB, LANES), jnp.float32),
            pltpu.VMEM((2 * SUB, LANES), jnp.float32),
        ],
        compiler_params=pltpu.CompilerParams(collective_id=0, has_side_effects=True),
    )(pair_blocks, window_decay, waveforms, segment_mask, jnp.asarray(high), jnp.asarray(low), jnp.asarray(twist),
      jnp.asarray(lag_table()))
    return stacked.reshape(1, stations, slots * stations, LAGS)


def solution(mesh):
    in_specs = (
        P("section", "sta", None, None),
        P("section", "sta", None),
        P("sta", None),
        P("section"),
    )
    out_specs = P("section", "sta", None, None)
    sizes = (mesh.shape["sta"], mesh.shape["section"])
    return jax.shard_map(
        functools.partial(body, sizes), mesh=mesh, in_specs=in_specs, out_specs=out_specs, check_vma=False
    )
```

```python
import functools
import math

import jax
import jax.numpy as jnp
import numpy as np
from jax import lax
from jax.experimental import pallas as pl
from jax.experimental.pallas import tpu as pltpu
from jax.sharding import PartitionSpec as P

MESH = pl.DeviceIdType.MESH
RADIX = 64
NF = 1024
LAGS = 384
SMOOTH_HALF = 32
LANES = 128
SUB = 8
EPSILON = 1e-05
NSAMP = RADIX * RADIX
FIRST = NSAMP // LANES
SLICES = FIRST // SUB
BINS = NF // FIRST


def dft_tables():
    b = np.arange(LANES)
    m = np.arange(BINS)
    phi = 2.0 * np.pi * ((b[:, None] * (m[None, :] + 2 * RADIX // FIRST)) % LANES) / LANES
    table = np.zeros((SLICES, 2, LANES, 2, BINS, SLICES))
    for q in range(SLICES):
        table[q, 0, :, 0, :, q] = np.cos(phi)
        table[q, 1, :, 0, :, q] = np.sin(phi)
        table[q, 0, :, 1, :, q] = -np.sin(phi)
        table[q, 1, :, 1, :, q] = np.cos(phi)
    table = (table / RADIX).reshape(SLICES * 2 * LANES, 2 * BINS * SLICES).astype(np.float32)
    high = table.astype(jnp.bfloat16)
    low = (table - high.astype(np.float32)).astype(jnp.bfloat16)
    turn = 2.0 * np.pi * np.arange(FIRST)[:, None] * b[None, :] / NSAMP
    twist = np.stack([np.cos(turn), np.sin(turn)], axis=1).astype(np.float32)
    return high, low, twist


def lag_table():
    f = SUB * np.arange(NF // SUB)[None, :] + np.arange(SUB)[:, None]
    shift = np.arange(LAGS) + NSAMP - LAGS // 2
    theta = 2.0 * np.pi * (((2 * RADIX + f)[:, :, None] * shift) % NSAMP) / NSAMP
    table = np.concatenate([np.cos(theta), -np.sin(theta)], axis=1) / math.sqrt(NF)
    return table.astype(np.float32).astype(jnp.bfloat16)


def real_dft(values):
    size = len(values)
    if size == 1:
        return [(values[0], None)]
    if size == 2:
        return [(values[0] + values[1], None), (values[0] - values[1], None)]
    even, odd = real_dft(values[0::2]), real_dft(values[1::2])
    half = size // 2
    out = [None] * (half + 1)
    for k in range(half // 2 + 1):
        er, ei = even[k]
        pr, pi = odd[k]
        if k == 0:
            out[0] = (er + pr, None)
            out[half] = (er - pr, None)
            continue
        if k * 4 == size:
            out[k] = (er, -pr)
            continue
        c, s = math.cos(2 * math.pi * k / size), math.sin(2 * math.pi * k / size)
        tr, ti = pr * c + pi * s, pi * c - pr * s
        out[k] = (er + tr, ei + ti)
        out[half - k] = (er - tr, ti - ei)
    return out


def spectrum(begin, count, x_ref, mask_ref, high_ref, low_ref, twist_ref, out_ref, y_ref, z_ref, w_ref):
    rows = count * SUB

    def first(st, _):
        pieces = [x_ref[0, begin + st, :, a * LANES:(a + 1) * LANES].astype(jnp.float32) for a in range(FIRST)]
        spread = real_dft(pieces)
        base = pl.multiple_of(st * SUB, SUB)
        for k1 in range(FIRST):
            re, im = spread[k1] if 2 * k1 <= FIRST else spread[FIRST - k1]
            c, s = twist_ref[k1, 0:1, :], twist_ref[k1, 1:2, :]
            if im is None:
                yr, yi = re * c, -(re * s)
            elif 2 * k1 <= FIRST:
                yr, yi = re * c + im * s, im * c - re * s
            else:
                yr, yi = re * c - im * s, -(im * c) - re * s
            q, p = k1 // SUB, k1 % SUB
            y_ref[pl.ds(p * rows + base, SUB), 2 * q * LANES:(2 * q + 1) * LANES] = yr
            y_ref[pl.ds(p * rows + base, SUB), (2 * q + 1) * LANES:(2 * q + 2) * LANES] = yi
        return 0

    lax.fori_loop(0, count, first, 0)
    y = y_ref[...]
    yh = y.astype(jnp.bfloat16)
    yl = (y - yh.astype(jnp.float32)).astype(jnp.bfloat16)
    dot = functools.partial(jnp.dot, preferred_element_type=jnp.float32)
    z_ref[...] = dot(yh, high_ref[...]) + dot(yl, high_ref[...]) + dot(yh, low_ref[...])
    reach = SMOOTH_HALF // SUB
    square = lax.broadcasted_iota(jnp.int32, (SUB, SUB), 0) == lax.broadcasted_iota(jnp.int32, (SUB, SUB), 1)

    def second(st, _):
        base = pl.multiple_of(st * SUB, SUB)
        lane = lax.broadcasted_iota(jnp.int32, (SUB, LANES), 1)

        def moved(v, d):
            inside = (lane + d >= 0) & (lane + d < LANES)
            return jnp.where(inside, pltpu.roll(v, (-d) % LANES, 1), 0.0)

        re = [z_ref[pl.ds(p * rows + base, SUB), 0:LANES] for p in range(SUB)]
        im = [z_ref[pl.ds(p * rows + base, SUB), LANES:2 * LANES] for p in range(SUB)]
        amp = [jnp.sqrt(re[p] * re[p] + im[p] * im[p]) for p in range(SUB)]
        pre = [amp[0]]
        for p in range(1, SUB):
            pre.append(pre[-1] + amp[p])
        suf = [amp[SUB - 1]]
        for p in range(SUB - 2, -1, -1):
            suf.insert(0, suf[0] + amp[p])
        middle = pre[-1]
        for d in range(1, reach):
            middle = middle + moved(pre[-1], d) + moved(pre[-1], -d)
        row = jnp.broadcast_to(mask_ref[0, pl.ds(begin + st, 1), :].astype(jnp.float32), (SUB, SUB))
        marks = jnp.sum(jnp.where(square, row, 0.0), axis=1, keepdims=True)
        for p in range(SUB):
            smooth = (middle + moved(suf[p], -reach) + moved(pre[p], reach)) / (2 * SMOOTH_HALF + 1)
            scale = marks / (smooth + EPSILON)
            w_ref[pl.ds(p, SUB, stride=2 * SUB), :] = re[p] * scale
            w_ref[pl.ds(SUB + p, SUB, stride=2 * SUB), :] = im[p] * scale
        out_ref[pl.ds(1 + begin * SUB + base, SUB)] = w_ref[...].reshape(SUB, 2 * SUB, LANES).astype(jnp.bfloat16)
        return 0

    lax.fori_loop(0, count, second, 0)


CHUNKS = 4


def correlate_kernel(n, windows, stations, slots, pair_ref, decay_ref, x_ref, mask_ref, high_ref,
                     low_ref, twist_ref, table_ref, out_ref, *scratch):
    bufs = scratch[:CHUNKS]
    (loc_ref, cr_ref, ci_ref, inv_ref, lag_ref, send_ref, got_ref, mine_ref, rate_ref, full_ref, rail_send, rail_recv,
     mate_send, mate_recv, lag_send, lag_recv, rate_send, rate_recv, own_ref, y_ref, z_ref, w_ref, row_ref) = scratch[CHUNKS:]
    me, window = lax.axis_index("sta"), lax.axis_index("section")
    length = n // 2
    core, place = lax.rem(me, 2), me // 2
    mate = place * 2 + 1 - core
    segments = SUB
    wide = stations // CHUNKS
    pairs = stations * slots
    mine_ref[...] = jnp.full(mine_ref.shape, decay_ref[0], jnp.float32)

    barrier = pltpu.get_barrier_semaphore()
    has_right, has_left = place < length - 1, place > 0

    def greet(peer):
        pl.semaphore_signal(barrier, inc=1, device_id=peer, device_id_type=MESH)

    greet({"sta": mate})
    for d in range(1, windows):
        greet({"section": lax.rem(window + d, windows)})

    @pl.when(has_right)
    def _():
        greet({"sta": me + 2})

    @pl.when(has_left)
    def _():
        greet({"sta": me - 2})

    def transform(c):
        spectrum(c * wide, wide, x_ref, mask_ref, high_ref, low_ref, twist_ref, own_ref, y_ref, z_ref, w_ref)

    row_ref[...] = jnp.zeros_like(row_ref)
    row_ref[0:stations, 0:SUB] = mask_ref[0].astype(jnp.float32)
    own_ref[0] = row_ref[...].astype(jnp.bfloat16)
    transform(0)
    pl.semaphore_wait(barrier, windows + jnp.where(has_right, 1, 0) + jnp.where(has_left, 1, 0))

    def span(c):
        return pl.ds(0 if c == 0 else 1 + c * wide * segments, wide * segments + (1 if c == 0 else 0))

    def rail(c, d, way):
        origin = me - 2 * way * d
        src = own_ref.at[span(c)] if d == 0 else bufs[c].at[origin]
        at = (c * length + d) * 2 + (1 + way) // 2
        return pltpu.make_async_remote_copy(
            src_ref=src, dst_ref=bufs[c].at[origin], send_sem=rail_send.at[at], recv_sem=rail_recv.at[at],
            device_id={"sta": me + 2 * way}, device_id_type=MESH)

    def landed(c, d, way):
        origin = me - 2 * way * d
        at = (c * length + d - 1) * 2 + (1 + way) // 2
        return pltpu.make_async_remote_copy(
            src_ref=bufs[c].at[origin], dst_ref=bufs[c].at[origin], send_sem=rail_send.at[at],
            recv_sem=rail_recv.at[at], device_id={"sta": me + 2 * way}, device_id_type=MESH)

    def across(c, origin_place, sender_core):
        origin = origin_place * 2 + sender_core
        at = c * length + origin_place
        return pltpu.make_async_remote_copy(
            src_ref=bufs[c].at[origin], dst_ref=bufs[c].at[origin], send_sem=mate_send.at[at],
            recv_sem=mate_recv.at[at], device_id={"sta": mate}, device_id_type=MESH)

    def own_across(c):
        at = c * length + place
        return pltpu.make_async_remote_copy(
            src_ref=own_ref.at[span(c)], dst_ref=bufs[c].at[me], send_sem=mate_send.at[at],
            recv_sem=mate_recv.at[at], device_id={"sta": mate}, device_id_type=MESH)

    def onward(way, d):
        return (place - way * d >= 0) & (place - way * d < length) & (place + way >= 0) & (place + way < length)

    def holds(way, d):
        return (place - way * d >= 0) & (place - way * d < length)

    def send_own(c):
        for way in (1, -1):
            @pl.when(onward(way, 0))
            def _():
                rail(c, 0, way).start()
        own_across(c).start()

    def later(c, d):
        return (
            pltpu.make_async_remote_copy(
                src_ref=send_ref.at[c], dst_ref=got_ref.at[window, c], send_sem=lag_send.at[d * CHUNKS + c],
                recv_sem=lag_recv.at[window * CHUNKS + c], device_id={"section": window + d}, device_id_type=MESH))

    def earlier(c, v):
        return pltpu.make_async_remote_copy(
            src_ref=send_ref.at[c], dst_ref=got_ref.at[v, c], send_sem=lag_send.at[c],
            recv_sem=lag_recv.at[v * CHUNKS + c], device_id={"section": v}, device_id_type=MESH)

    def rate_later(d):
        return pltpu.make_async_remote_copy(
            src_ref=mine_ref, dst_ref=rate_ref.at[window], send_sem=rate_send.at[d],
            recv_sem=rate_recv.at[window], device_id={"section": window + d}, device_id_type=MESH)

    def rate_earlier(v):
        return pltpu.make_async_remote_copy(
            src_ref=mine_ref, dst_ref=rate_ref.at[v], send_sem=rate_send.at[0],
            recv_sem=rate_recv.at[v], device_id={"section": v}, device_id_type=MESH)

    ahead = 2
    send_own(0)
    for d in range(1, windows):
        @pl.when(window + d < windows)
        def _():
            rate_later(d).start()
    for c in range(1, CHUNKS):
        transform(c)
        bufs[c][me] = own_ref[span(c)]
        if c < ahead:
            send_own(c)
    bufs[0][me] = own_ref[span(0)]
    loc_ref[...] = own_ref[1:1 + stations * segments].astype(jnp.float32)

    def combine(c):
        rows = wide * pairs
        full_ref[...] = jnp.zeros_like(full_ref)
        for v in range(windows - 1):
            @pl.when(v < window)
            def _():
                if c == 0:
                    rate_earlier(v).wait_recv()
                earlier(c, v).wait_recv()
                full_ref[...] = full_ref[...] * rate_ref[v, 0:1, 0:1] + got_ref[v, c].astype(jnp.float32)
        total = full_ref[...] * mine_ref[0:1, 0:1] + lag_ref[c * rows:(c + 1) * rows, :]
        for jj in range(wide):
            for part in range(LAGS // LANES):
                cols = slice(part * LANES, (part + 1) * LANES)
                inv_ref[1 + part, pl.ds(c * wide + jj, pairs, stride=stations), :] = total[jj * pairs:(jj + 1) * pairs, cols]

    def relay(c):
        for d in range(1, length):
            for way in (1, -1):
                @pl.when(holds(way, d))
                def _():
                    landed(c, d, way).wait_recv()

                @pl.when(onward(way, d))
                def _():
                    rail(c, d, way).start()

                @pl.when(holds(way, d))
                def _():
                    across(c, place - way * d, core).start()
            if d == 1 and c + ahead < CHUNKS:
                send_own(c + ahead)

    relay(0)
    for c in range(CHUNKS):
        if c + 1 < CHUNKS:
            relay(c + 1)
        for origin in range(length):
            across(c, origin, 1 - core).wait_recv()
        first = 1 if c == 0 else 0
        if c == 0:
            mine = own_ref[0].astype(jnp.float32)
            for k in range(slots):
                theirs = bufs[0][pair_ref[0, k], 0].astype(jnp.float32)[0:stations]
                for i in range(stations):
                    count = jnp.sum(mine[i:i + 1] * theirs, axis=1, keepdims=True)
                    at = (i * slots + k) * stations
                    inv_ref[0, at:at + stations, :] = jnp.broadcast_to(1.0 / jnp.maximum(count, 1.0), (stations, LANES))

        def pair(t, _):
            k, jj = t // wide, lax.rem(t, wide)
            block = pair_ref[0, k]
            other = [bufs[c][block, first + jj * segments + s].astype(jnp.float32) for s in range(segments)]
            for i in range(stations):
                re = im = None
                for s in range(segments):
                    ar, ai = loc_ref[i * segments + s, 0:SUB, :], loc_ref[i * segments + s, SUB:2 * SUB, :]
                    br, bi = other[s][0:SUB], other[s][SUB:2 * SUB]
                    tr, ti = ar * br + ai * bi, ar * bi - ai * br
                    re, im = (tr, ti) if re is None else (re + tr, im + ti)
                at = pl.ds(pl.multiple_of((jj * pairs + i * slots + k) * SUB, SUB), SUB)
                cr_ref[at, :] = re
                ci_ref[at, :] = im
            return 0

        lax.fori_loop(0, slots * wide, pair, 0)
        rows = wide * pairs
        acc = None
        for p in range(SUB):
            at = pl.ds(p, rows, stride=SUB)
            lhs = jnp.concatenate([cr_ref[at, :], ci_ref[at, :]], axis=1).astype(jnp.bfloat16)
            term = jnp.dot(lhs, table_ref[p], preferred_element_type=jnp.float32)
            acc = term if acc is None else acc + term
        for jj in range(wide):
            inv = inv_ref[0, pl.ds(c * wide + jj, pairs, stride=stations), :]
            value = acc[jj * pairs:(jj + 1) * pairs] * jnp.concatenate([inv] * (LAGS // LANES), axis=1)
            lag_ref[c * rows + jj * pairs:c * rows + (jj + 1) * pairs, :] = value
            send_ref[c, jj * pairs:(jj + 1) * pairs, :] = value.astype(jnp.bfloat16)
        for d in range(1, windows):
            @pl.when(window + d < windows)
            def _():
                later(c, d).start()
        if c > 0:
            combine(c - 1)
    combine(CHUNKS - 1)
    for part in range(LAGS // LANES):
        out_ref[:, part * LANES:(part + 1) * LANES] = inv_ref[1 + part].astype(jnp.bfloat16)
    for c in range(CHUNKS):
        for d in range(length):
            for way in (1, -1):
                @pl.when(onward(way, d))
                def _():
                    rail(c, d, way).wait_send()
        for origin in range(length):
            across(c, origin, core).wait_send()
        for d in range(1, windows):
            @pl.when(window + d < windows)
            def _():
                later(c, d).wait_send()
    for d in range(1, windows):
        @pl.when(window + d < windows)
        def _():
            rate_later(d).wait_send()


def body(sizes, waveforms, segment_mask, pair_blocks, window_decay):
    n, windows = sizes
    stations, segments = waveforms.shape[1], waveforms.shape[2]
    slots = pair_blocks.shape[1]
    rows = stations * segments
    high, low, twist = dft_tables()
    vmem = pl.BlockSpec(memory_space=pltpu.VMEM)
    smem = pl.BlockSpec(memory_space=pltpu.SMEM)
    dma = pltpu.SemaphoreType.DMA
    total = stations * slots * stations
    part = total // CHUNKS
    length = n // 2
    bufs = [
        pltpu.VMEM((n, rows // CHUNKS + (1 if c == 0 else 0), 2 * SUB, LANES), jnp.bfloat16) for c in range(CHUNKS)
    ]
    stacked = pl.pallas_call(
        functools.partial(correlate_kernel, n, windows, stations, slots),
        name="correlate",
        out_shape=jax.ShapeDtypeStruct((total, LAGS), jnp.bfloat16),
        in_specs=[smem, smem] + [vmem] * 6,
        out_specs=vmem,
        scratch_shapes=bufs + [
            pltpu.VMEM((rows, 2 * SUB, LANES), jnp.float32),
            pltpu.VMEM((part * SUB, LANES), jnp.float32),
            pltpu.VMEM((part * SUB, LANES), jnp.float32),
            pltpu.VMEM((1 + LAGS // LANES, total, LANES), jnp.float32),
            pltpu.VMEM((total, LAGS), jnp.float32),
            pltpu.VMEM((CHUNKS, part, LAGS), jnp.bfloat16),
            pltpu.VMEM((windows, CHUNKS, part, LAGS), jnp.bfloat16),
            pltpu.VMEM((SUB, LANES), jnp.float32),
            pltpu.VMEM((windows, SUB, LANES), jnp.float32),
            pltpu.VMEM((part, LAGS), jnp.float32),
            dma((2 * CHUNKS * length,)), dma((2 * CHUNKS * length,)),
            dma((CHUNKS * length,)), dma((CHUNKS * length,)),
            dma((windows * CHUNKS,)), dma((windows * CHUNKS,)),
            dma((windows,)), dma((windows,)),
            pltpu.VMEM((1 + rows, 2 * SUB, LANES), jnp.bfloat16),
            pltpu.VMEM((SUB * rows // CHUNKS, SLICES * 2 * LANES), jnp.float32),
            pltpu.VMEM((SUB * rows // CHUNKS, 2 * LANES), jnp.float32),
            pltpu.VMEM((SUB * 2 * SUB, LANES), jnp.float32),
            pltpu.VMEM((2 * SUB, LANES), jnp.float32),
        ],
        compiler_params=pltpu.CompilerParams(collective_id=0, has_side_effects=True),
    )(pair_blocks, window_decay, waveforms, segment_mask, jnp.asarray(high), jnp.asarray(low), jnp.asarray(twist),
      jnp.asarray(lag_table()))
    return stacked.reshape(1, stations, slots * stations, LAGS)


def solution(mesh):
    in_specs = (
        P("section", "sta", None, None),
        P("section", "sta", None),
        P("sta", None),
        P("section"),
    )
    out_specs = P("section", "sta", None, None)
    sizes = (mesh.shape["sta"], mesh.shape["section"])
    return jax.shard_map(
        functools.partial(body, sizes), mesh=mesh, in_specs=in_specs, out_specs=out_specs, check_vma=False
    )
```
